1024 devices in a mesh: dp: 8 (over x), ctx: 16 (over y, core), tp: 8 (over z).
Axes of the slice: x: 8, y: 8, z: 8, core: 2. Of those that a mesh axis runs over, the one named last changes fastest.
Arguments:
- query_rows: bfloat16 [8, 6144, 8192], P('dp', 'ctx', 'tp'), may hold values from -2.5 to 2.5
- key_rows: bfloat16 [8, 6144, 1024], P('dp', 'ctx', 'tp'), may hold values from -2.5 to 2.5
- value_rows: bfloat16 [8, 6144, 1024], P('dp', 'ctx', 'tp'), may hold values from -6 to 6
- out_grad: bfloat16 [8, 6144, 8192], P('dp', 'ctx', 'tp'), may hold values from -6 to 6
- assistant: int32 [8, 48], P('dp'), may hold values from 0 to 1, as said below
- turn_first: int32 [8, 48], P('dp'), may hold values from 0 to 47, as said below
Outputs:
- query_grad: bfloat16 [8, 6144, 8192], P('dp', 'ctx', 'tp')
- key_grad: bfloat16 [8, 6144, 1024], P('dp', 'ctx', 'tp')
- value_grad: bfloat16 [8, 6144, 1024], P('dp', 'ctx', 'tp')
The draws below stay inside these ranges and needn't reach their ends.
Inputs may be any that keep to these rules, and one draw needn't show every extreme that they name: Among the 3 blocks at positions d * 3 to d * 3 + 2 at most 2 are assistant blocks, and in every sequence some such group holds exactly 2. Turns are runs of whole blocks: turn_first never falls, equals the block's own index where a turn begins, and q - 4 <= turn_first[q] <= q; in every sequence some block has q - turn_first[q] = 4.
All inputs are finite; a program needn't handle non-finite values.
Results may differ from the reference program's by a relative error of at most 0.005.
Values may be sent and summed in bfloat16 or wider, within the bound.
A program may use at most 32 MiB of HBM per device.

```python
import math
import jax
import jax.numpy as jnp
from jax import lax

BLK = 128
QH = 8
HD = 128
KVH = 8
BATCH = 8
SEQ = 6144
NB_DEV = 3
NBLK = 48
REACH = 4
A_MAX = 2


def draw_assistant(key, part):
    groups = NBLK // NB_DEV

    def one_sequence(seq_key):
        count_key, forced_key, order_key = jax.random.split(seq_key, 3)
        counts = jax.random.randint(count_key, (groups,), 0, A_MAX + 1)
        forced = jax.random.randint(forced_key, (), 0, groups)
        counts = jnp.where(jnp.arange(groups) == forced, A_MAX, counts)
        ranking = jax.vmap(lambda inner_key: jax.random.permutation(inner_key, NB_DEV))(jax.random.split(order_key, groups))
        return (ranking < counts[:, None]).astype(jnp.int32).reshape(NBLK)
    return jax.vmap(one_sequence)(jax.random.split(jax.random.fold_in(key, 11), BATCH))


def draw_turn_first(key, part):

    def one_sequence(seq_key):
        lengths = jax.random.randint(seq_key, (NBLK,), 1, REACH + 2)
        lengths = lengths.at[0].set(REACH + 1)
        starts = jnp.cumsum(lengths) - lengths
        block_ids = jnp.arange(NBLK, dtype=jnp.int32)
        is_start = jnp.any(starts[None, :] == block_ids[:, None], axis=1)
        return lax.cummax(jnp.where(is_start, block_ids, 0), axis=0).astype(jnp.int32)
    return jax.vmap(one_sequence)(jax.random.split(jax.random.fold_in(key, 23), BATCH))


def level_of(stream_key, shape, shards, smallest, high):
    def one(position, blocks):
        draws = jax.random.uniform(jax.random.fold_in(jax.random.fold_in(stream_key, 6), position), (blocks,), jnp.float32, smallest / len(shards), high / len(shards))
        return jnp.repeat(jnp.exp(draws), shape[position] // blocks).reshape((-1,) + (1,) * (len(shape) - position - 1))

    loudness = one(*shards[0])
    for cut in shards[1:]:
        loudness = loudness * one(*cut)
    return loudness


def centred(key, extent, spread, limit, cuts=(), kind=jnp.bfloat16):
    array = spread * jax.random.normal(key, extent, jnp.float32)
    if cuts:
        array = array * level_of(key, extent, cuts, -0.22, 0.18)
    return jnp.clip(array, -limit, limit).astype(kind)


def setup_inputs(seed: int = 0) -> dict:
    key_of = jax.random.split(jax.random.key(seed), 7)
    return {
        "query_rows": centred(key_of[0], (BATCH, SEQ, KVH * QH * HD), 1.0, 2.5, ((0, 8), (1, 16), (2, 8))),
        "key_rows": centred(key_of[1], (BATCH, SEQ, KVH * HD), 1.0, 2.5, ((0, 8), (1, 16), (2, 8))),
        "value_rows": centred(key_of[2], (BATCH, SEQ, KVH * HD), 1.0, 6.0, ((0, 8), (1, 16), (2, 8))),
        "out_grad": centred(key_of[3], (BATCH, SEQ, KVH * QH * HD), 1.0, 6.0, ((0, 8), (1, 16), (2, 8))),
        "assistant": draw_assistant(jax.random.fold_in(key_of[6], 71), 0),
        "turn_first": draw_turn_first(jax.random.fold_in(key_of[6], 71), 0),
    }


def reference(query_rows, key_rows, value_rows, out_grad, assistant, turn_first):
    scale_factor = 1.0 / math.sqrt(HD)
    key_span = (REACH + 1) * BLK
    pad_rows = REACH * BLK
    highest = lax.Precision.HIGHEST

    def one_sequence(seq_args):
        query_seq, key_seq, value_seq, grad_seq, assist_mark, turn_start = seq_args
        query_blocks = query_seq.reshape(NBLK, BLK, KVH, QH, HD)
        grad_blocks = grad_seq.reshape(NBLK, BLK, KVH, QH, HD)
        key_padded = jnp.concatenate([jnp.zeros((pad_rows, KVH * HD), key_seq.dtype), key_seq], 0).reshape(-1, KVH, HD)
        value_padded = jnp.concatenate([jnp.zeros((pad_rows, KVH * HD), value_seq.dtype), value_seq], 0).reshape(-1, KVH, HD)

        def live_block(block_index):
            query_block = lax.dynamic_index_in_dim(query_blocks, block_index, 0, keepdims=False).astype(jnp.float32)
            grad_block = lax.dynamic_index_in_dim(grad_blocks, block_index, 0, keepdims=False).astype(jnp.float32)
            key_window = lax.dynamic_slice_in_dim(key_padded, block_index * BLK, key_span, 0).astype(jnp.float32)
            value_window = lax.dynamic_slice_in_dim(value_padded, block_index * BLK, key_span, 0).astype(jnp.float32)
            scores = jnp.einsum('bghd,kgd->ghbk', query_block, key_window, precision=highest)
            key_pos = (block_index - REACH) * BLK + jnp.arange(key_span, dtype=jnp.int32)
            query_pos = block_index * BLK + jnp.arange(BLK, dtype=jnp.int32)
            turn_begin = lax.dynamic_index_in_dim(turn_start, block_index, 0, keepdims=False) * BLK
            allowed = (key_pos[None, :] >= turn_begin) & (key_pos[None, :] <= query_pos[:, None])
            weights = jnp.where(allowed, jnp.exp(scores * scale_factor), 0.0)
            attention = weights / lax.optimization_barrier(jnp.sum(weights, axis=3, keepdims=True))
            prob_grad = jnp.einsum('bghd,kgd->ghbk', grad_block, value_window, precision=highest)
            row_delta = lax.optimization_barrier(jnp.sum(attention * prob_grad, axis=3, keepdims=True))
            score_grad = (attention * (prob_grad - row_delta)).astype(jnp.bfloat16).astype(jnp.float32)
            attention_low = attention.astype(jnp.bfloat16).astype(jnp.float32)
            query_grad = (scale_factor * jnp.einsum('ghbk,kgd->bghd', score_grad, key_window, precision=highest)).astype(jnp.bfloat16)
            key_part = scale_factor * jnp.einsum('ghbk,bghd->kgd', score_grad, query_block, precision=highest)
            value_part = jnp.einsum('ghbk,bghd->kgd', attention_low, grad_block, precision=highest)
            return (query_grad, key_part, value_part)

        def dead_block(block_index):
            return (jnp.zeros((BLK, KVH, QH, HD), jnp.bfloat16), jnp.zeros((key_span, KVH, HD), jnp.float32), jnp.zeros((key_span, KVH, HD), jnp.float32))

        def block_step(carried, block_index):
            key_acc, value_acc = carried
            is_live = lax.dynamic_index_in_dim(assist_mark, block_index, 0, keepdims=False) == 1
            query_grad, key_part, value_part = lax.cond(is_live, live_block, dead_block, block_index)
            offset = block_index * BLK
            key_acc = lax.dynamic_update_slice_in_dim(key_acc, lax.dynamic_slice_in_dim(key_acc, offset, key_span, 0) + key_part, offset, 0)
            value_acc = lax.dynamic_update_slice_in_dim(value_acc, lax.dynamic_slice_in_dim(value_acc, offset, key_span, 0) + value_part, offset, 0)
            return ((key_acc, value_acc), query_grad)
        start_acc = jnp.zeros(((NBLK + REACH) * BLK, KVH, HD), jnp.float32)
        (key_acc, value_acc), query_all = lax.scan(block_step, (start_acc, start_acc), jnp.arange(NBLK, dtype=jnp.int32))
        query_seq_grad = query_all.reshape(SEQ, KVH * QH * HD)
        key_seq_grad = key_acc[pad_rows:].reshape(SEQ, KVH * HD).astype(jnp.bfloat16)
        value_seq_grad = value_acc[pad_rows:].reshape(SEQ, KVH * HD).astype(jnp.bfloat16)
        return (query_seq_grad, key_seq_grad, value_seq_grad)
    query_grad, key_grad, value_grad = lax.map(one_sequence, (query_rows, key_rows, value_rows, out_grad, assistant, turn_first))
    return (query_grad, key_grad, value_grad)
```

```python
import math

import jax
import jax.numpy as jnp
from jax import lax
from jax.experimental import pallas as pl
from jax.experimental.pallas import tpu as pltpu
from jax.sharding import PartitionSpec as P

BLK = 128
QH = 8
NB = 3
REACH = 4
WIN = REACH + NB
SLOT = QH * BLK
UNIT = 2 * BLK
UNITS = SLOT // UNIT
MESH = pl.DeviceIdType.MESH
F32 = jnp.float32
BF16 = jnp.bfloat16


def dot_nt(a, b):
    return lax.dot_general(a, b, (((1,), (1,)), ((), ())), preferred_element_type=F32)


def dot_nn(a, b):
    return lax.dot_general(a, b, (((1,), (0,)), ((), ())), preferred_element_type=F32)


def sub_sum(x):
    return jnp.sum(x.reshape(x.shape[0] // 8, 8, x.shape[1]), axis=0)


def kernel(
    ranks,
    assist,
    first,
    q_hbm,
    k_hbm,
    v_hbm,
    g_hbm,
    dq_out,
    dk_out,
    dv_out,
    q_in,
    g_in,
    win_k,
    win_v,
    q_all,
    g_all,
    k_t,
    w_buf,
    d_buf,
    ds_buf,
    l_buf,
    e_buf,
    acc_k,
    acc_v,
    out_k,
    out_v,
    near_k,
    near_v,
    far_k,
    far_v,
    dq_slot,
    in_sem,
    fs_sem,
    fr_sem,
    bs_sem,
    br_sem,
):
    me = lax.axis_index("ctx")
    scale = 1.0 / math.sqrt(BLK)
    base = me * NB
    halo = REACH * BLK

    local = [
        pltpu.make_async_copy(k_hbm, win_k.at[pl.ds(halo, NB * BLK)], in_sem.at[0]),
        pltpu.make_async_copy(v_hbm, win_v.at[pl.ds(halo, NB * BLK)], in_sem.at[1]),
        pltpu.make_async_copy(q_hbm, q_in, in_sem.at[2]),
        pltpu.make_async_copy(g_hbm, g_in, in_sem.at[3]),
    ]
    for copy in local:
        copy.start()

    def halo_copy(array, block, window, away, slot):
        src = (k_hbm, v_hbm)[array].at[pl.ds(block * BLK, BLK)]
        dst = (win_k, win_v)[array].at[pl.ds(window * BLK, BLK)]
        return pltpu.make_async_remote_copy(
            src_ref=src,
            dst_ref=dst,
            send_sem=fs_sem.at[slot],
            recv_sem=fr_sem.at[slot],
            device_id={"ctx": me + away},
            device_id_type=MESH,
        )

    halo_copies = []
    for window in (0, 1, 2, 3):
        away = 2 if window == 0 else 1
        block = NB - 1 if window == 0 else window - 1
        for array in (0, 1):
            halo_copies.append(
                (away, window, halo_copy(array, block, window, away, 2 * window + array))
            )

    def back_copy(array, window, slot):
        src = (out_k, out_v)[array].at[pl.ds(window * BLK, BLK)]
        if window == 0:
            dst = (far_k, far_v)[array]
        else:
            dst = (near_k, near_v)[array].at[pl.ds((window - 1) * BLK, BLK)]
        away = 2 if window == 0 else 1
        return pltpu.make_async_remote_copy(
            src_ref=src,
            dst_ref=dst,
            send_sem=bs_sem.at[slot],
            recv_sem=br_sem.at[slot],
            device_id={"ctx": me - away},
            device_id_type=MESH,
        )

    back_copies = []
    for window in (0, 1, 2, 3):
        away = 2 if window == 0 else 1
        for array in (0, 1):
            back_copies.append((away, window, back_copy(array, window, 2 * window + array)))

    barrier = pltpu.get_barrier_semaphore()
    for away in (1, 2):

        @pl.when(me >= away)
        def _():
            pl.semaphore_signal(
                barrier, inc=1, device_id={"ctx": me - away}, device_id_type=MESH
            )

        @pl.when(me + away < ranks)
        def _():
            pl.semaphore_signal(
                barrier, inc=1, device_id={"ctx": me + away}, device_id_type=MESH
            )

    pl.semaphore_wait(barrier, jnp.minimum(me, 2) + jnp.minimum(ranks - 1 - me, 2))

    for away, window, copy in halo_copies:

        @pl.when(me + away < ranks)
        def _():
            copy.start()

    for away, window, _ in halo_copies[::2]:

        @pl.when(me < away)
        def _():
            zero = jnp.zeros((BLK, BLK), BF16)
            win_k[window * BLK : (window + 1) * BLK, :] = zero
            win_v[window * BLK : (window + 1) * BLK, :] = zero

    for away, window, _ in back_copies[::2]:

        @pl.when(me + away >= ranks)
        def _():
            zero = jnp.zeros((BLK, BLK), BF16)
            if window == 0:
                far_k[...] = zero
                far_v[...] = zero
            else:
                near_k[(window - 1) * BLK : window * BLK, :] = zero
                near_v[(window - 1) * BLK : window * BLK, :] = zero

    mark = [assist[0, base + i] for i in range(NB)]
    turn = [first[0, base + i] for i in range(NB)]
    head_is_first = mark[0] == 1
    tail_is_last = mark[2] == 1
    slot_block = (jnp.where(head_is_first, 0, 1), jnp.where(tail_is_last, 2, 1))
    slot_turn = (
        jnp.where(head_is_first, turn[0], turn[1]),
        jnp.where(tail_is_last, turn[2], turn[1]),
    )
    slot_live = (
        jnp.maximum(mark[0], mark[1]),
        jnp.maximum(mark[2], mark[0] * mark[1]),
    )

    def valid(slot, window):
        seen = (base - REACH + window >= slot_turn[slot]) & (slot_live[slot] == 1)
        return jnp.where(seen, jnp.float32(1.0), jnp.float32(0.0))

    l_buf[...] = jnp.zeros_like(l_buf)
    e_buf[...] = jnp.zeros_like(e_buf)
    acc_k[...] = jnp.zeros_like(acc_k)
    acc_v[...] = jnp.zeros_like(acc_v)
    for copy in local:
        copy.wait()

    for slot in (0, 1):
        low = slice(slot * BLK, (slot + 1) * BLK)
        high = slice((slot + 1) * BLK, (slot + 2) * BLK)
        for head in range(QH):
            at = slot * SLOT + head * BLK
            cols = slice(head * BLK, (head + 1) * BLK)
            is_low = slot_block[slot] == slot
            q_all[at : at + BLK, :] = jnp.where(is_low, q_in[low, cols], q_in[high, cols])
            g_all[at : at + BLK, :] = jnp.where(is_low, g_in[low, cols], g_in[high, cols])

    ahead = (lax.broadcasted_iota(jnp.int32, (BLK, UNIT), 1) % BLK) - lax.broadcasted_iota(
        jnp.int32, (BLK, UNIT), 0
    )

    def weigh(slot, windows):
        def step(u, carry):
            unit = slot * UNITS + u
            at = pl.ds(pl.multiple_of(unit * UNIT, UNIT), UNIT)
            q_t = q_all[at, :]
            g_t = g_all[at, :]
            total = l_buf[unit]
            total_e = e_buf[unit]
            for window in windows:
                keys = slice(window * BLK, (window + 1) * BLK)
                scores = dot_nt(win_k[keys, :], q_t)
                prob_grad = dot_nt(win_v[keys, :], g_t)
                w = jnp.exp2(scores * (scale * math.log2(math.e)))
                if window >= REACH:
                    w = jnp.where(ahead >= (window - REACH - slot_block[slot]) * BLK, w, 0.0)
                w_buf[unit, keys, :] = w
                d_buf[unit, keys, :] = prob_grad
                on = valid(slot, window)
                total = total + on * sub_sum(w)
                total_e = total_e + on * sub_sum(w * prob_grad)
            l_buf[unit] = total
            e_buf[unit] = total_e
            return carry

        lax.fori_loop(0, UNITS, step, 0)

    own = ((4, 5), (4, 5, 6))
    other = ((0, 1, 2, 3), (1, 2, 3))
    for slot in (0, 1):
        weigh(slot, own[slot])

    for away, window, copy in halo_copies:

        @pl.when(me >= away)
        def _():
            copy.wait_recv()

    for slot in (0, 1):
        weigh(slot, other[slot])

    def finish(unit):
        total = jnp.sum(l_buf[unit], axis=0, keepdims=True)
        total_e = jnp.sum(e_buf[unit], axis=0, keepdims=True)
        inverse = jnp.where(total > 0.0, 1.0 / total, 0.0)
        return inverse, total_e * inverse

    def grads(slot, unit, windows):
        at = pl.ds(pl.multiple_of(unit * UNIT, UNIT), UNIT)
        q_t = q_all[at, :]
        g_t = g_all[at, :]
        inverse, delta = finish(unit)
        for window in windows:
            keys = slice(window * BLK, (window + 1) * BLK)
            attention = w_buf[unit, keys, :] * (inverse * valid(slot, window))
            score_grad = (attention * (d_buf[unit, keys, :] - delta)).astype(BF16)
            ds_buf[unit, keys, :] = score_grad
            acc_k[keys, :] += dot_nn(score_grad, q_t)
            acc_v[keys, :] += dot_nn(attention.astype(BF16), g_t)

    for slot in (0, 1):

        def far_step(u, carry):
            grads(slot, slot * UNITS + u, other[slot])
            return carry

        lax.fori_loop(0, UNITS, far_step, 0)

    out_k[...] = (acc_k[:halo, :] * scale).astype(BF16)
    out_v[...] = acc_v[:halo, :].astype(BF16)
    for away, window, copy in back_copies:

        @pl.when(me >= away)
        def _():
            copy.start()

    for window in range(WIN):
        keys = slice(window * BLK, (window + 1) * BLK)
        k_t[:, keys] = win_k[keys, :].T

    for slot in (0, 1):

        def own_step(u, carry):
            unit = slot * UNITS + u
            grads(slot, unit, own[slot])
            keys = slice(slot * BLK, (slot + WIN - 1) * BLK)
            part = dot_nn(k_t[:, keys], ds_buf[unit, keys, :]) * scale
            both = jnp.concatenate([part[:, :BLK].T, part[:, BLK:].T], axis=1)
            cols = pl.ds(pl.multiple_of(u * UNIT, UNIT), UNIT)
            dq_slot[slot, :, cols] = both.astype(BF16)
            return carry

        lax.fori_loop(0, UNITS, own_step, 0)

    for block in range(NB):
        rows = slice(block * BLK, (block + 1) * BLK)
        use = [(slot_block[s] == block) & (slot_live[s] == 1) for s in (0, 1)]
        value = jnp.where(use[1], dq_slot[1], jnp.zeros((), BF16))
        dq_out[rows, :] = jnp.where(use[0], dq_slot[0], value)

    for away, window, copy in back_copies:

        @pl.when(me + away < ranks)
        def _():
            copy.wait_recv()

    total_k = acc_k[halo:, :] * scale + near_k[...].astype(F32)
    total_v = acc_v[halo:, :] + near_v[...].astype(F32)
    last = (NB - 1) * BLK
    dk_out[:last, :] = total_k[:last].astype(BF16)
    dv_out[:last, :] = total_v[:last].astype(BF16)
    dk_out[last:, :] = (total_k[last:] + far_k[...].astype(F32)).astype(BF16)
    dv_out[last:, :] = (total_v[last:] + far_v[...].astype(F32)).astype(BF16)

    for away, window, copy in halo_copies:

        @pl.when(me + away < ranks)
        def _():
            copy.wait_send()

    for away, window, copy in back_copies:

        @pl.when(me >= away)
        def _():
            copy.wait_send()


def per_device(ranks, query_rows, key_rows, value_rows, out_grad, assistant, turn_first):
    rows = NB * BLK
    hbm = pl.BlockSpec(memory_space=pltpu.HBM)
    smem = pl.BlockSpec(memory_space=pltpu.SMEM)
    vmem = pl.BlockSpec(memory_space=pltpu.VMEM)
    units = 2 * UNITS
    scratch = [
        pltpu.VMEM((rows, SLOT), BF16),
        pltpu.VMEM((rows, SLOT), BF16),
        pltpu.VMEM((WIN * BLK, BLK), BF16),
        pltpu.VMEM((WIN * BLK, BLK), BF16),
        pltpu.VMEM((2 * SLOT, BLK), BF16),
        pltpu.VMEM((2 * SLOT, BLK), BF16),
        pltpu.VMEM((BLK, WIN * BLK), BF16),
        pltpu.VMEM((units, WIN * BLK, UNIT), F32),
        pltpu.VMEM((units, WIN * BLK, UNIT), F32),
        pltpu.VMEM((units, WIN * BLK, UNIT), BF16),
        pltpu.VMEM((units, 8, UNIT), F32),
        pltpu.VMEM((units, 8, UNIT), F32),
        pltpu.VMEM((WIN * BLK, BLK), F32),
        pltpu.VMEM((WIN * BLK, BLK), F32),
        pltpu.VMEM((REACH * BLK, BLK), BF16),
        pltpu.VMEM((REACH * BLK, BLK), BF16),
        pltpu.VMEM((rows, BLK), BF16),
        pltpu.VMEM((rows, BLK), BF16),
        pltpu.VMEM((BLK, BLK), BF16),
        pltpu.VMEM((BLK, BLK), BF16),
        pltpu.VMEM((2, BLK, SLOT), BF16),
        pltpu.SemaphoreType.DMA((4,)),
        pltpu.SemaphoreType.DMA((8,)),
        pltpu.SemaphoreType.DMA((8,)),
        pltpu.SemaphoreType.DMA((8,)),
        pltpu.SemaphoreType.DMA((8,)),
    ]

    blocks = [
        pltpu.with_memory_space_constraint(x[0], pltpu.HBM)
        for x in (query_rows, key_rows, value_rows, out_grad)
    ]

    def body(*refs):
        kernel(ranks, *refs)

    dq, dk, dv = pl.pallas_call(
        body,
        out_shape=(
            jax.ShapeDtypeStruct((rows, SLOT), BF16),
            jax.ShapeDtypeStruct((rows, BLK), BF16),
            jax.ShapeDtypeStruct((rows, BLK), BF16),
        ),
        in_specs=[smem, smem, hbm, hbm, hbm, hbm],
        out_specs=(vmem, vmem, vmem),
        scratch_shapes=scratch,
        compiler_params=pltpu.CompilerParams(
            collective_id=0, has_side_effects=True, vmem_limit_bytes=40 * 1024 * 1024
        ),
        name="attention_backward",
    )(assistant, turn_first, *blocks)
    return dq[None], dk[None], dv[None]


def solution(mesh):
    ranks = mesh.shape["ctx"]

    def step(*arrays):
        return per_device(ranks, *arrays)

    wide = P("dp", "ctx", "tp")
    return jax.shard_map(
        step,
        mesh=mesh,
        in_specs=(wide, wide, wide, wide, P("dp", None), P("dp", None)),
        out_specs=(wide, wide, wide),
        check_vma=False,
    )
```

```python
import math

import jax
import jax.numpy as jnp
from jax import lax
from jax.experimental import pallas as pl
from jax.experimental.pallas import tpu as pltpu
from jax.sharding import PartitionSpec as P

BLK = 128
QH = 8
NB = 3
REACH = 4
WIN = REACH + NB
SLOT = QH * BLK
UNIT = 2 * BLK
UNITS = SLOT // UNIT
MESH = pl.DeviceIdType.MESH
F32 = jnp.float32
BF16 = jnp.bfloat16


def dot_nt(a, b):
    return lax.dot_general(a, b, (((1,), (1,)), ((), ())), preferred_element_type=F32)


def dot_nn(a, b):
    return lax.dot_general(a, b, (((1,), (0,)), ((), ())), preferred_element_type=F32)


def sub_sum(x):
    return jnp.sum(x.reshape(x.shape[0] // 8, 8, x.shape[1]), axis=0)


def kernel(
    ranks,
    assist_hbm,
    first_hbm,
    q_hbm,
    k_hbm,
    v_hbm,
    g_hbm,
    dq_out,
    dk_out,
    dv_out,
    q_in,
    g_in,
    win_k,
    win_v,
    q_all,
    g_all,
    k_t,
    w_buf,
    d_buf,
    ds_buf,
    l_buf,
    e_buf,
    acc_k,
    acc_v,
    out_k,
    out_v,
    near_k,
    near_v,
    far_k,
    far_v,
    dq_slot,
    assist,
    first,
    in_sem,
    fs_sem,
    fr_sem,
    bs_sem,
    br_sem,
):
    me = lax.axis_index("ctx")
    scale = 1.0 / math.sqrt(BLK)
    base = me * NB
    halo = REACH * BLK

    local = [
        pltpu.make_async_copy(k_hbm, win_k.at[pl.ds(halo, NB * BLK)], in_sem.at[0]),
        pltpu.make_async_copy(v_hbm, win_v.at[pl.ds(halo, NB * BLK)], in_sem.at[1]),
        pltpu.make_async_copy(q_hbm, q_in, in_sem.at[2]),
        pltpu.make_async_copy(g_hbm, g_in, in_sem.at[3]),
        pltpu.make_async_copy(assist_hbm, assist, in_sem.at[4]),
        pltpu.make_async_copy(first_hbm, first, in_sem.at[5]),
    ]
    for copy in local:
        copy.start()

    def halo_copy(array, block, window, away, slot):
        src = (k_hbm, v_hbm)[array].at[pl.ds(block * BLK, BLK)]
        dst = (win_k, win_v)[array].at[pl.ds(window * BLK, BLK)]
        return pltpu.make_async_remote_copy(
            src_ref=src,
            dst_ref=dst,
            send_sem=fs_sem.at[slot],
            recv_sem=fr_sem.at[slot],
            device_id={"ctx": me + away},
            device_id_type=MESH,
        )

    halo_copies = []
    for window in (0, 1, 2, 3):
        away = 2 if window == 0 else 1
        block = NB - 1 if window == 0 else window - 1
        for array in (0, 1):
            halo_copies.append(
                (away, window, halo_copy(array, block, window, away, 2 * window + array))
            )

    def back_copy(array, window, slot):
        src = (out_k, out_v)[array].at[pl.ds(window * BLK, BLK)]
        if window == 0:
            dst = (far_k, far_v)[array]
        else:
            dst = (near_k, near_v)[array].at[pl.ds((window - 1) * BLK, BLK)]
        away = 2 if window == 0 else 1
        return pltpu.make_async_remote_copy(
            src_ref=src,
            dst_ref=dst,
            send_sem=bs_sem.at[slot],
            recv_sem=br_sem.at[slot],
            device_id={"ctx": me - away},
            device_id_type=MESH,
        )

    back_copies = []
    for window in (0, 1, 2, 3):
        away = 2 if window == 0 else 1
        for array in (0, 1):
            back_copies.append((away, window, back_copy(array, window, 2 * window + array)))

    barrier = pltpu.get_barrier_semaphore()
    for away in (1, 2):

        @pl.when(me >= away)
        def _():
            pl.semaphore_signal(
                barrier, inc=1, device_id={"ctx": me - away}, device_id_type=MESH
            )

        @pl.when(me + away < ranks)
        def _():
            pl.semaphore_signal(
                barrier, inc=1, device_id={"ctx": me + away}, device_id_type=MESH
            )

    pl.semaphore_wait(barrier, jnp.minimum(me, 2) + jnp.minimum(ranks - 1 - me, 2))

    for away, window, copy in halo_copies:

        @pl.when(me + away < ranks)
        def _():
            copy.start()

    for away, window, _ in halo_copies[::2]:

        @pl.when(me < away)
        def _():
            zero = jnp.zeros((BLK, BLK), BF16)
            win_k[window * BLK : (window + 1) * BLK, :] = zero
            win_v[window * BLK : (window + 1) * BLK, :] = zero

    for away, window, _ in back_copies[::2]:

        @pl.when(me + away >= ranks)
        def _():
            zero = jnp.zeros((BLK, BLK), BF16)
            if window == 0:
                far_k[...] = zero
                far_v[...] = zero
            else:
                near_k[(window - 1) * BLK : window * BLK, :] = zero
                near_v[(window - 1) * BLK : window * BLK, :] = zero

    for copy in local:
        copy.wait()

    mark = [assist[0, base + i] for i in range(NB)]
    turn = [first[0, base + i] for i in range(NB)]
    head_is_first = mark[0] == 1
    tail_is_last = mark[2] == 1
    slot_block = (jnp.where(head_is_first, 0, 1), jnp.where(tail_is_last, 2, 1))
    slot_turn = (
        jnp.where(head_is_first, turn[0], turn[1]),
        jnp.where(tail_is_last, turn[2], turn[1]),
    )
    slot_live = (
        jnp.maximum(mark[0], mark[1]),
        jnp.maximum(mark[2], mark[0] * mark[1]),
    )

    def valid(slot, window):
        seen = (base - REACH + window >= slot_turn[slot]) & (slot_live[slot] == 1)
        return jnp.where(seen, jnp.float32(1.0), jnp.float32(0.0))

    for slot in (0, 1):
        low = slice(slot * BLK, (slot + 1) * BLK)
        high = slice((slot + 1) * BLK, (slot + 2) * BLK)
        for head in range(QH):
            at = slot * SLOT + head * BLK
            cols = slice(head * BLK, (head + 1) * BLK)
            is_low = slot_block[slot] == slot
            q_all[at : at + BLK, :] = jnp.where(is_low, q_in[low, cols], q_in[high, cols])
            g_all[at : at + BLK, :] = jnp.where(is_low, g_in[low, cols], g_in[high, cols])

    ahead = (lax.broadcasted_iota(jnp.int32, (BLK, UNIT), 1) % BLK) - lax.broadcasted_iota(
        jnp.int32, (BLK, UNIT), 0
    )

    def weigh(slot, windows, opens):
        for unit in range(slot * UNITS, (slot + 1) * UNITS):
            at = slice(unit * UNIT, (unit + 1) * UNIT)
            q_t = q_all[at, :]
            g_t = g_all[at, :]
            total = None if opens else l_buf[unit]
            total_e = None if opens else e_buf[unit]
            for window in windows:
                keys = slice(window * BLK, (window + 1) * BLK)
                scores = dot_nt(win_k[keys, :], q_t)
                prob_grad = dot_nt(win_v[keys, :], g_t)
                w = jnp.exp2(scores * (scale * math.log2(math.e)))
                if window >= REACH:
                    w = jnp.where(ahead >= (window - REACH - slot_block[slot]) * BLK, w, 0.0)
                w_buf[unit, keys, :] = w
                d_buf[unit, keys, :] = prob_grad
                on = valid(slot, window)
                more = on * sub_sum(w)
                more_e = on * sub_sum(w * prob_grad)
                total = more if total is None else total + more
                total_e = more_e if total_e is None else total_e + more_e
            l_buf[unit] = total
            e_buf[unit] = total_e

    def finish(unit):
        total = jnp.sum(l_buf[unit], axis=0, keepdims=True)
        total_e = jnp.sum(e_buf[unit], axis=0, keepdims=True)
        inverse = jnp.where(total > 0.0, 1.0 / total, 0.0)
        return inverse, total_e * inverse

    written = set()

    def grads(slot, windows):
        for unit in range(slot * UNITS, (slot + 1) * UNITS):
            at = slice(unit * UNIT, (unit + 1) * UNIT)
            q_t = q_all[at, :]
            g_t = g_all[at, :]
            inverse, delta = finish(unit)
            for window in windows:
                keys = slice(window * BLK, (window + 1) * BLK)
                attention = w_buf[unit, keys, :] * (inverse * valid(slot, window))
                score_grad = (attention * (d_buf[unit, keys, :] - delta)).astype(BF16)
                ds_buf[unit, keys, :] = score_grad
                part_k = dot_nn(score_grad, q_t)
                part_v = dot_nn(attention.astype(BF16), g_t)
                if window in written:
                    part_k = acc_k[keys, :] + part_k
                    part_v = acc_v[keys, :] + part_v
                written.add(window)
                acc_k[keys, :] = part_k
                acc_v[keys, :] = part_v

    def received(copies, windows):
        for away, window, copy in copies:
            if window in windows:

                @pl.when(me >= away)
                def _():
                    copy.wait_recv()

    def give_back(windows):
        for window in windows:
            keys = slice(window * BLK, (window + 1) * BLK)
            out_k[keys, :] = (acc_k[keys, :] * scale).astype(BF16)
            out_v[keys, :] = acc_v[keys, :].astype(BF16)
        for away, window, copy in back_copies:
            if window in windows:

                @pl.when(me >= away)
                def _():
                    copy.start()

    weigh(0, (4, 5), True)
    weigh(1, (4, 5, 6), True)
    received(halo_copies, (1, 2, 3))
    weigh(1, (1, 2, 3), False)
    weigh(0, (1, 2, 3), False)
    grads(1, (1, 2, 3))
    received(halo_copies, (0,))
    weigh(0, (0,), False)
    grads(0, (1, 2, 3))
    give_back((1, 2, 3))
    grads(0, (0,))
    give_back((0,))

    for window in range(WIN):
        keys = slice(window * BLK, (window + 1) * BLK)
        k_t[:, keys] = win_k[keys, :].T
    for slot, windows in ((0, (4, 5)), (1, (4, 5, 6))):
        grads(slot, windows)
        keys = slice(slot * BLK, (slot + WIN - 1) * BLK)
        for u in range(UNITS):
            part = dot_nn(k_t[:, keys], ds_buf[slot * UNITS + u, keys, :]) * scale
            both = jnp.concatenate([part[:, :BLK].T, part[:, BLK:].T], axis=1)
            dq_slot[slot, :, u * UNIT : (u + 1) * UNIT] = both.astype(BF16)

    for block in range(NB):
        rows = slice(block * BLK, (block + 1) * BLK)
        use = [(slot_block[s] == block) & (slot_live[s] == 1) for s in (0, 1)]
        value = jnp.where(use[1], dq_slot[1], jnp.zeros((), BF16))
        dq_out[rows, :] = jnp.where(use[0], dq_slot[0], value)

    for away, window, copy in back_copies:

        @pl.when(me + away < ranks)
        def _():
            copy.wait_recv()

    total_k = acc_k[halo:, :] * scale + near_k[...].astype(F32)
    total_v = acc_v[halo:, :] + near_v[...].astype(F32)
    last = (NB - 1) * BLK
    dk_out[:last, :] = total_k[:last].astype(BF16)
    dv_out[:last, :] = total_v[:last].astype(BF16)
    dk_out[last:, :] = (total_k[last:] + far_k[...].astype(F32)).astype(BF16)
    dv_out[last:, :] = (total_v[last:] + far_v[...].astype(F32)).astype(BF16)

    for away, window, copy in halo_copies:

        @pl.when(me + away < ranks)
        def _():
            copy.wait_send()

    for away, window, copy in back_copies:

        @pl.when(me >= away)
        def _():
            copy.wait_send()


def put_out(dq_in, dk_in, dv_in, dq_hbm, dk_hbm, dv_hbm, sem):
    copies = [
        pltpu.make_async_copy(dq_in, dq_hbm, sem.at[0]),
        pltpu.make_async_copy(dk_in, dk_hbm, sem.at[1]),
        pltpu.make_async_copy(dv_in, dv_hbm, sem.at[2]),
    ]
    for copy in copies:
        copy.start()
    for copy in copies:
        copy.wait()


def per_device(ranks, query_rows, key_rows, value_rows, out_grad, assistant, turn_first):
    rows = NB * BLK
    hbm = pl.BlockSpec(memory_space=pltpu.HBM)
    vmem = pl.BlockSpec(memory_space=pltpu.VMEM)
    units = 2 * UNITS
    scratch = [
        pltpu.VMEM((rows, SLOT), BF16),
        pltpu.VMEM((rows, SLOT), BF16),
        pltpu.VMEM((WIN * BLK, BLK), BF16),
        pltpu.VMEM((WIN * BLK, BLK), BF16),
        pltpu.VMEM((2 * SLOT, BLK), BF16),
        pltpu.VMEM((2 * SLOT, BLK), BF16),
        pltpu.VMEM((BLK, WIN * BLK), BF16),
        pltpu.VMEM((units, WIN * BLK, UNIT), F32),
        pltpu.VMEM((units, WIN * BLK, UNIT), F32),
        pltpu.VMEM((units, WIN * BLK, UNIT), BF16),
        pltpu.VMEM((units, 8, UNIT), F32),
        pltpu.VMEM((units, 8, UNIT), F32),
        pltpu.VMEM((WIN * BLK, BLK), F32),
        pltpu.VMEM((WIN * BLK, BLK), F32),
        pltpu.VMEM((REACH * BLK, BLK), BF16),
        pltpu.VMEM((REACH * BLK, BLK), BF16),
        pltpu.VMEM((rows, BLK), BF16),
        pltpu.VMEM((rows, BLK), BF16),
        pltpu.VMEM((BLK, BLK), BF16),
        pltpu.VMEM((BLK, BLK), BF16),
        pltpu.VMEM((2, BLK, SLOT), BF16),
        pltpu.SMEM((1, assistant.shape[1]), jnp.int32),
        pltpu.SMEM((1, assistant.shape[1]), jnp.int32),
        pltpu.SemaphoreType.DMA((6,)),
        pltpu.SemaphoreType.DMA((8,)),
        pltpu.SemaphoreType.DMA((8,)),
        pltpu.SemaphoreType.DMA((8,)),
        pltpu.SemaphoreType.DMA((8,)),
    ]

    blocks = [
        pltpu.with_memory_space_constraint(x, pltpu.HBM)
        for x in (assistant, turn_first, query_rows[0], key_rows[0], value_rows[0], out_grad[0])
    ]

    def body(*refs):
        kernel(ranks, *refs)

    shapes = (
        jax.ShapeDtypeStruct((rows, SLOT), BF16),
        jax.ShapeDtypeStruct((rows, BLK), BF16),
        jax.ShapeDtypeStruct((rows, BLK), BF16),
    )
    held = pl.pallas_call(
        body,
        out_shape=shapes,
        in_specs=[hbm, hbm, hbm, hbm, hbm, hbm],
        out_specs=(vmem, vmem, vmem),
        scratch_shapes=scratch,
        compiler_params=pltpu.CompilerParams(
            collective_id=0, has_side_effects=True, vmem_limit_bytes=40 * 1024 * 1024
        ),
        name="attention_backward",
    )(*blocks)
    dq, dk, dv = pl.pallas_call(
        put_out,
        out_shape=shapes,
        in_specs=[vmem, vmem, vmem],
        out_specs=(hbm, hbm, hbm),
        scratch_shapes=[pltpu.SemaphoreType.DMA((3,))],
        compiler_params=pltpu.CompilerParams(vmem_limit_bytes=4 * 1024 * 1024),
        name="put_out",
    )(*held)
    return dq[None], dk[None], dv[None]


def solution(mesh):
    ranks = mesh.shape["ctx"]

    def step(*arrays):
        return per_device(ranks, *arrays)

    wide = P("dp", "ctx", "tp")
    return jax.shard_map(
        step,
        mesh=mesh,
        in_specs=(wide, wide, wide, wide, P("dp", None), P("dp", None)),
        out_specs=(wide, wide, wide),
        check_vma=False,
    )
```

```python
import math

import jax
import jax.numpy as jnp
from jax import lax
from jax.experimental import pallas as pl
from jax.experimental.pallas import tpu as pltpu
from jax.sharding import PartitionSpec as P

BLK = 128
QH = 8
NB = 3
REACH = 4
WIN = REACH + NB
SLOT = QH * BLK
UNIT = 2 * BLK
UNITS = SLOT // UNIT
MESH = pl.DeviceIdType.MESH
F32 = jnp.float32
BF16 = jnp.bfloat16


def dot_nt(a, b):
    return lax.dot_general(a, b, (((1,), (1,)), ((), ())), preferred_element_type=F32)


def dot_nn(a, b):
    return lax.dot_general(a, b, (((1,), (0,)), ((), ())), preferred_element_type=F32)


def sub_sum(x):
    return jnp.sum(x.reshape(x.shape[0] // 8, 8, x.shape[1]), axis=0)


def kernel(
    ranks,
    assist_hbm,
    first_hbm,
    q_hbm,
    k_hbm,
    v_hbm,
    g_hbm,
    dq_out,
    dk_out,
    dv_out,
    q_in,
    g_in,
    win_k,
    win_v,
    q_all,
    g_all,
    k_t,
    w_buf,
    d_buf,
    ds_buf,
    l_buf,
    e_buf,
    acc_k,
    acc_v,
    out_k,
    out_v,
    near_k,
    near_v,
    far_k,
    far_v,
    assist,
    first,
    in_sem,
    fs_sem,
    fr_sem,
    bs_sem,
    br_sem,
):
    me = lax.axis_index("ctx")
    scale = 1.0 / math.sqrt(BLK)
    base = me * NB
    halo = REACH * BLK

    local = [
        pltpu.make_async_copy(k_hbm, win_k.at[pl.ds(halo, NB * BLK)], in_sem.at[0]),
        pltpu.make_async_copy(v_hbm, win_v.at[pl.ds(halo, NB * BLK)], in_sem.at[1]),
        pltpu.make_async_copy(q_hbm, q_in, in_sem.at[2]),
        pltpu.make_async_copy(g_hbm, g_in, in_sem.at[3]),
        pltpu.make_async_copy(assist_hbm, assist, in_sem.at[4]),
        pltpu.make_async_copy(first_hbm, first, in_sem.at[5]),
    ]
    for copy in local:
        copy.start()

    def halo_copy(array, block, window, away, slot):
        src = (k_hbm, v_hbm)[array].at[pl.ds(block * BLK, BLK)]
        dst = (win_k, win_v)[array].at[pl.ds(window * BLK, BLK)]
        return pltpu.make_async_remote_copy(
            src_ref=src,
            dst_ref=dst,
            send_sem=fs_sem.at[slot],
            recv_sem=fr_sem.at[slot],
            device_id={"ctx": me + away},
            device_id_type=MESH,
        )

    halo_copies = []
    for window in (0, 1, 2, 3):
        away = 2 if window == 0 else 1
        block = NB - 1 if window == 0 else window - 1
        for array in (0, 1):
            halo_copies.append(
                (away, window, halo_copy(array, block, window, away, 2 * window + array))
            )

    def back_copy(array, window, slot):
        src = (out_k, out_v)[array].at[pl.ds(window * BLK, BLK)]
        if window == 0:
            dst = (far_k, far_v)[array]
        else:
            dst = (near_k, near_v)[array].at[pl.ds((window - 1) * BLK, BLK)]
        away = 2 if window == 0 else 1
        return pltpu.make_async_remote_copy(
            src_ref=src,
            dst_ref=dst,
            send_sem=bs_sem.at[slot],
            recv_sem=br_sem.at[slot],
            device_id={"ctx": me - away},
            device_id_type=MESH,
        )

    back_copies = []
    for window in (0, 1, 2, 3):
        away = 2 if window == 0 else 1
        for array in (0, 1):
            back_copies.append((away, window, back_copy(array, window, 2 * window + array)))

    barrier = pltpu.get_barrier_semaphore()
    for away in (1, 2):

        @pl.when(me >= away)
        def _():
            pl.semaphore_signal(
                barrier, inc=1, device_id={"ctx": me - away}, device_id_type=MESH
            )

    @pl.when(me < ranks - 1)
    def _():
        pl.semaphore_wait(barrier, jnp.minimum(ranks - 1 - me, 2))

    for away, window, copy in halo_copies:

        @pl.when(me + away < ranks)
        def _():
            copy.start()

    for away, window, _ in halo_copies[::2]:

        @pl.when(me < away)
        def _():
            zero = jnp.zeros((BLK, BLK), BF16)
            win_k[window * BLK : (window + 1) * BLK, :] = zero
            win_v[window * BLK : (window + 1) * BLK, :] = zero

    for away, window, _ in back_copies[::2]:

        @pl.when(me + away >= ranks)
        def _():
            zero = jnp.zeros((BLK, BLK), BF16)
            if window == 0:
                far_k[...] = zero
                far_v[...] = zero
            else:
                near_k[(window - 1) * BLK : window * BLK, :] = zero
                near_v[(window - 1) * BLK : window * BLK, :] = zero

    for copy in local:
        copy.wait()

    mark = [assist[0, base + i] for i in range(NB)]
    turn = [first[0, base + i] for i in range(NB)]
    head_is_first = mark[0] == 1
    tail_is_last = mark[2] == 1
    slot_block = (jnp.where(head_is_first, 0, 1), jnp.where(tail_is_last, 2, 1))
    slot_turn = (
        jnp.where(head_is_first, turn[0], turn[1]),
        jnp.where(tail_is_last, turn[2], turn[1]),
    )
    slot_live = (
        jnp.maximum(mark[0], mark[1]),
        jnp.maximum(mark[2], mark[0] * mark[1]),
    )

    def valid(slot, window):
        seen = (base - REACH + window >= slot_turn[slot]) & (slot_live[slot] == 1)
        return jnp.where(seen, jnp.float32(1.0), jnp.float32(0.0))

    for slot in (0, 1):
        low = slice(slot * BLK, (slot + 1) * BLK)
        high = slice((slot + 1) * BLK, (slot + 2) * BLK)
        for head in range(QH):
            at = slot * SLOT + head * BLK
            cols = slice(head * BLK, (head + 1) * BLK)
            is_low = slot_block[slot] == slot
            q_all[at : at + BLK, :] = jnp.where(is_low, q_in[low, cols], q_in[high, cols])
            g_all[at : at + BLK, :] = jnp.where(is_low, g_in[low, cols], g_in[high, cols])

    ahead = (lax.broadcasted_iota(jnp.int32, (BLK, UNIT), 1) % BLK) - lax.broadcasted_iota(
        jnp.int32, (BLK, UNIT), 0
    )

    def weigh(slot, windows, opens):
        for unit in range(slot * UNITS, (slot + 1) * UNITS):
            at = slice(unit * UNIT, (unit + 1) * UNIT)
            q_t = q_all[at, :]
            g_t = g_all[at, :]
            total = None if opens else l_buf[unit]
            total_e = None if opens else e_buf[unit]
            for window in windows:
                keys = slice(window * BLK, (window + 1) * BLK)
                scores = dot_nt(win_k[keys, :], q_t)
                prob_grad = dot_nt(win_v[keys, :], g_t)
                w = jnp.exp2(scores * (scale * math.log2(math.e)))
                if window >= REACH:
                    w = jnp.where(ahead >= (window - REACH - slot_block[slot]) * BLK, w, 0.0)
                w_buf[unit, keys, :] = w
                d_buf[unit, keys, :] = prob_grad
                on = valid(slot, window)
                more = on * sub_sum(w)
                more_e = on * sub_sum(w * prob_grad)
                total = more if total is None else total + more
                total_e = more_e if total_e is None else total_e + more_e
            l_buf[unit] = total
            e_buf[unit] = total_e

    finished = {}

    def finish(unit):
        if unit not in finished:
            finished[unit] = normalise(unit)
        return finished[unit]

    def normalise(unit):
        total = jnp.sum(l_buf[unit], axis=0, keepdims=True)
        total_e = jnp.sum(e_buf[unit], axis=0, keepdims=True)
        inverse = jnp.where(total > 0.0, 1.0 / total, 0.0)
        return inverse, total_e * inverse

    written = set()

    def grads(slot, windows):
        for unit in range(slot * UNITS, (slot + 1) * UNITS):
            at = slice(unit * UNIT, (unit + 1) * UNIT)
            q_t = q_all[at, :]
            g_t = g_all[at, :]
            inverse, delta = finish(unit)
            for window in windows:
                keys = slice(window * BLK, (window + 1) * BLK)
                attention = w_buf[unit, keys, :] * (inverse * valid(slot, window))
                score_grad = (attention * (d_buf[unit, keys, :] - delta)).astype(BF16)
                ds_buf[unit, keys, :] = score_grad
                part_k = dot_nn(score_grad, q_t)
                part_v = dot_nn(attention.astype(BF16), g_t)
                if window in written:
                    part_k = acc_k[keys, :] + part_k
                    part_v = acc_v[keys, :] + part_v
                written.add(window)
                acc_k[keys, :] = part_k
                acc_v[keys, :] = part_v

    def received(copies, windows):
        for away, window, copy in copies:
            if window in windows:

                @pl.when(me >= away)
                def _():
                    copy.wait_recv()

    def give_back(windows):
        for window in windows:
            keys = slice(window * BLK, (window + 1) * BLK)
            out_k[keys, :] = (acc_k[keys, :] * scale).astype(BF16)
            out_v[keys, :] = acc_v[keys, :].astype(BF16)
        for away, window, copy in back_copies:
            if window in windows:

                @pl.when(me >= away)
                def _():
                    copy.start()

    weigh(0, (4, 5), True)
    weigh(1, (4, 5, 6), True)
    received(halo_copies, (1, 2, 3))
    weigh(1, (1, 2, 3), False)
    weigh(0, (1, 2, 3), False)
    grads(1, (1, 2, 3))
    received(halo_copies, (0,))
    weigh(0, (0,), False)
    for windows in ((1,), (2,), (3,), (0,)):
        grads(0, windows)
        give_back(windows)

    for window in range(WIN):
        keys = slice(window * BLK, (window + 1) * BLK)
        k_t[:, keys] = win_k[keys, :].T
    zero = jnp.zeros((), BF16)
    for slot, windows in ((0, (4, 5)), (1, (4, 5, 6))):
        grads(slot, windows)
        keys = slice(slot * BLK, (slot + WIN - 1) * BLK)
        for u in range(UNITS):
            part = dot_nn(k_t[:, keys], ds_buf[slot * UNITS + u, keys, :]) * scale
            both = jnp.concatenate([part[:, :BLK].T, part[:, BLK:].T], axis=1).astype(BF16)
            cols = slice(u * UNIT, (u + 1) * UNIT)
            is_low = slot_block[slot] == slot
            if slot == 0:
                dq_out[:BLK, cols] = jnp.where(is_low, both, zero)
                dq_out[BLK : 2 * BLK, cols] = jnp.where(is_low, zero, both)
            else:
                middle = dq_out[BLK : 2 * BLK, cols]
                take = is_low & (slot_live[1] == 1)
                dq_out[BLK : 2 * BLK, cols] = jnp.where(take, both, middle)
                dq_out[2 * BLK :, cols] = jnp.where(is_low, zero, both)

    for away, window, copy in back_copies:

        @pl.when(me + away < ranks)
        def _():
            copy.wait_recv()

    total_k = acc_k[halo:, :] * scale + near_k[...].astype(F32)
    total_v = acc_v[halo:, :] + near_v[...].astype(F32)
    last = (NB - 1) * BLK
    dk_out[:last, :] = total_k[:last].astype(BF16)
    dv_out[:last, :] = total_v[:last].astype(BF16)
    dk_out[last:, :] = (total_k[last:] + far_k[...].astype(F32)).astype(BF16)
    dv_out[last:, :] = (total_v[last:] + far_v[...].astype(F32)).astype(BF16)

    for away, window, copy in halo_copies:

        @pl.when(me + away < ranks)
        def _():
            copy.wait_send()

    for away, window, copy in back_copies:

        @pl.when(me >= away)
        def _():
            copy.wait_send()


def put_out(dq_in, dk_in, dv_in, dq_hbm, dk_hbm, dv_hbm, sem):
    copies = [
        pltpu.make_async_copy(dq_in, dq_hbm, sem.at[0]),
        pltpu.make_async_copy(dk_in, dk_hbm, sem.at[1]),
        pltpu.make_async_copy(dv_in, dv_hbm, sem.at[2]),
    ]
    for copy in copies:
        copy.start()
    for copy in copies:
        copy.wait()


def per_device(ranks, query_rows, key_rows, value_rows, out_grad, assistant, turn_first):
    rows = NB * BLK
    hbm = pl.BlockSpec(memory_space=pltpu.HBM)
    vmem = pl.BlockSpec(memory_space=pltpu.VMEM)
    units = 2 * UNITS
    scratch = [
        pltpu.VMEM((rows, SLOT), BF16),
        pltpu.VMEM((rows, SLOT), BF16),
        pltpu.VMEM((WIN * BLK, BLK), BF16),
        pltpu.VMEM((WIN * BLK, BLK), BF16),
        pltpu.VMEM((2 * SLOT, BLK), BF16),
        pltpu.VMEM((2 * SLOT, BLK), BF16),
        pltpu.VMEM((BLK, WIN * BLK), BF16),
        pltpu.VMEM((units, WIN * BLK, UNIT), F32),
        pltpu.VMEM((units, WIN * BLK, UNIT), F32),
        pltpu.VMEM((units, WIN * BLK, UNIT), BF16),
        pltpu.VMEM((units, 8, UNIT), F32),
        pltpu.VMEM((units, 8, UNIT), F32),
        pltpu.VMEM((WIN * BLK, BLK), F32),
        pltpu.VMEM((WIN * BLK, BLK), F32),
        pltpu.VMEM((REACH * BLK, BLK), BF16),
        pltpu.VMEM((REACH * BLK, BLK), BF16),
        pltpu.VMEM((rows, BLK), BF16),
        pltpu.VMEM((rows, BLK), BF16),
        pltpu.VMEM((BLK, BLK), BF16),
        pltpu.VMEM((BLK, BLK), BF16),
        pltpu.SMEM((1, assistant.shape[1]), jnp.int32),
        pltpu.SMEM((1, assistant.shape[1]), jnp.int32),
        pltpu.SemaphoreType.DMA((6,)),
        pltpu.SemaphoreType.DMA((8,)),
        pltpu.SemaphoreType.DMA((8,)),
        pltpu.SemaphoreType.DMA((8,)),
        pltpu.SemaphoreType.DMA((8,)),
    ]

    blocks = [
        pltpu.with_memory_space_constraint(x, pltpu.HBM)
        for x in (assistant, turn_first, query_rows[0], key_rows[0], value_rows[0], out_grad[0])
    ]

    def body(*refs):
        kernel(ranks, *refs)

    shapes = (
        jax.ShapeDtypeStruct((rows, SLOT), BF16),
        jax.ShapeDtypeStruct((rows, BLK), BF16),
        jax.ShapeDtypeStruct((rows, BLK), BF16),
    )
    held = pl.pallas_call(
        body,
        out_shape=shapes,
        in_specs=[hbm, hbm, hbm, hbm, hbm, hbm],
        out_specs=(vmem, vmem, vmem),
        scratch_shapes=scratch,
        compiler_params=pltpu.CompilerParams(
            collective_id=0, has_side_effects=True, vmem_limit_bytes=40 * 1024 * 1024
        ),
        name="attention_backward",
    )(*blocks)
    dq, dk, dv = pl.pallas_call(
        put_out,
        out_shape=shapes,
        in_specs=[vmem, vmem, vmem],
        out_specs=(hbm, hbm, hbm),
        scratch_shapes=[pltpu.SemaphoreType.DMA((3,))],
        compiler_params=pltpu.CompilerParams(vmem_limit_bytes=4 * 1024 * 1024),
        name="put_out",
    )(*held)
    return dq[None], dk[None], dv[None]


def solution(mesh):
    ranks = mesh.shape["ctx"]

    def step(*arrays):
        return per_device(ranks, *arrays)

    wide = P("dp", "ctx", "tp")
    return jax.shard_map(
        step,
        mesh=mesh,
        in_specs=(wide, wide, wide, wide, P("dp", None), P("dp", None)),
        out_specs=(wide, wide, wide),
        check_vma=False,
    )
```

```python
import math

import jax
import jax.numpy as jnp
from jax import lax
from jax.experimental import pallas as pl
from jax.experimental.pallas import tpu as pltpu
from jax.sharding import PartitionSpec as P

BLK = 128
QH = 8
NB = 3
REACH = 4
WIN = REACH + NB
SLOT = QH * BLK
UNIT = 2 * BLK
UNITS = SLOT // UNIT
MESH = pl.DeviceIdType.MESH
F32 = jnp.float32
BF16 = jnp.bfloat16


def dot_nt(a, b):
    return lax.dot_general(a, b, (((1,), (1,)), ((), ())), preferred_element_type=F32)


def dot_nn(a, b):
    return lax.dot_general(a, b, (((1,), (0,)), ((), ())), preferred_element_type=F32)


def sub_sum(x):
    return jnp.sum(x.reshape(x.shape[0] // 8, 8, x.shape[1]), axis=0)


def kernel(
    ranks,
    assist_hbm,
    first_hbm,
    q_hbm,
    k_hbm,
    v_hbm,
    g_hbm,
    dq_out,
    dk_out,
    dv_out,
    q_in,
    g_in,
    win_k,
    win_v,
    q_all,
    g_all,
    k_t,
    w_buf,
    d_buf,
    ds_buf,
    l_buf,
    e_buf,
    acc_k,
    acc_v,
    out_k,
    out_v,
    near_k,
    near_v,
    far_k,
    far_v,
    assist,
    first,
    in_sem,
    fs_sem,
    fr_sem,
    bs_sem,
    br_sem,
):
    me = lax.axis_index("ctx")
    scale = 1.0 / math.sqrt(BLK)
    base = me * NB
    halo = REACH * BLK

    local = [
        pltpu.make_async_copy(k_hbm, win_k.at[pl.ds(halo, NB * BLK)], in_sem.at[0]),
        pltpu.make_async_copy(v_hbm, win_v.at[pl.ds(halo, NB * BLK)], in_sem.at[1]),
        pltpu.make_async_copy(q_hbm, q_in, in_sem.at[2]),
        pltpu.make_async_copy(g_hbm, g_in, in_sem.at[3]),
        pltpu.make_async_copy(assist_hbm, assist, in_sem.at[4]),
        pltpu.make_async_copy(first_hbm, first, in_sem.at[5]),
    ]
    def halo_copy(array, block, window, away, slot):
        src = (k_hbm, v_hbm)[array].at[pl.ds(block * BLK, BLK)]
        dst = (win_k, win_v)[array].at[pl.ds(window * BLK, BLK)]
        return pltpu.make_async_remote_copy(
            src_ref=src,
            dst_ref=dst,
            send_sem=fs_sem.at[slot],
            recv_sem=fr_sem.at[slot],
            device_id={"ctx": me + away},
            device_id_type=MESH,
        )

    halo_copies = []
    for window in (0, 1, 2, 3):
        away = 2 if window == 0 else 1
        block = NB - 1 if window == 0 else window - 1
        for array in (0, 1):
            halo_copies.append(
                (away, window, array, halo_copy(array, block, window, away, 2 * window + array))
            )

    def back_copy(array, window, slot):
        src = (out_k, out_v)[array].at[pl.ds(window * BLK, BLK)]
        if window == 0:
            dst = (far_k, far_v)[array]
        else:
            dst = (near_k, near_v)[array].at[pl.ds((window - 1) * BLK, BLK)]
        away = 2 if window == 0 else 1
        return pltpu.make_async_remote_copy(
            src_ref=src,
            dst_ref=dst,
            send_sem=bs_sem.at[slot],
            recv_sem=br_sem.at[slot],
            device_id={"ctx": me - away},
            device_id_type=MESH,
        )

    back_copies = []
    for window in (0, 1, 2, 3):
        away = 2 if window == 0 else 1
        for array in (0, 1):
            slot = 2 * window + array
            back_copies.append((away, window, array, back_copy(array, window, slot)))

    barrier = pltpu.get_barrier_semaphore()
    for away in (1, 2):

        @pl.when(me >= away)
        def _():
            pl.semaphore_signal(
                barrier, inc=1, device_id={"ctx": me - away}, device_id_type=MESH
            )

    @pl.when(me < ranks - 1)
    def _():
        pl.semaphore_wait(barrier, jnp.minimum(ranks - 1 - me, 2))

    for away, window, array, copy in halo_copies:

        @pl.when(me + away < ranks)
        def _():
            copy.start()

    for copy in local:
        copy.start()

    for away, window, _, _ in halo_copies[::2]:

        @pl.when(me < away)
        def _():
            zero = jnp.zeros((BLK, BLK), BF16)
            win_k[window * BLK : (window + 1) * BLK, :] = zero
            win_v[window * BLK : (window + 1) * BLK, :] = zero

    for away, window, _, _ in back_copies[::2]:

        @pl.when(me + away >= ranks)
        def _():
            zero = jnp.zeros((BLK, BLK), BF16)
            if window == 0:
                far_k[...] = zero
                far_v[...] = zero
            else:
                near_k[(window - 1) * BLK : window * BLK, :] = zero
                near_v[(window - 1) * BLK : window * BLK, :] = zero

    for copy in local:
        copy.wait()

    mark = [assist[0, base + i] for i in range(NB)]
    turn = [first[0, base + i] for i in range(NB)]
    head_is_first = mark[0] == 1
    tail_is_last = mark[2] == 1
    slot_block = (jnp.where(head_is_first, 0, 1), jnp.where(tail_is_last, 2, 1))
    slot_turn = (
        jnp.where(head_is_first, turn[0], turn[1]),
        jnp.where(tail_is_last, turn[2], turn[1]),
    )
    slot_live = (
        jnp.maximum(mark[0], mark[1]),
        jnp.maximum(mark[2], mark[0] * mark[1]),
    )

    def valid(slot, window):
        seen = (base - REACH + window >= slot_turn[slot]) & (slot_live[slot] == 1)
        return jnp.where(seen, jnp.float32(1.0), jnp.float32(0.0))

    for slot in (0, 1):
        low = slice(slot * BLK, (slot + 1) * BLK)
        high = slice((slot + 1) * BLK, (slot + 2) * BLK)
        for head in range(QH):
            at = slot * SLOT + head * BLK
            cols = slice(head * BLK, (head + 1) * BLK)
            is_low = slot_block[slot] == slot
            q_all[at : at + BLK, :] = jnp.where(is_low, q_in[low, cols], q_in[high, cols])
            g_all[at : at + BLK, :] = jnp.where(is_low, g_in[low, cols], g_in[high, cols])

    ahead = (lax.broadcasted_iota(jnp.int32, (BLK, UNIT), 1) % BLK) - lax.broadcasted_iota(
        jnp.int32, (BLK, UNIT), 0
    )

    def weigh(slot, windows, opens):
        for unit in range(slot * UNITS, (slot + 1) * UNITS):
            at = slice(unit * UNIT, (unit + 1) * UNIT)
            q_t = q_all[at, :]
            g_t = g_all[at, :]
            total = None if opens else l_buf[unit]
            total_e = None if opens else e_buf[unit]
            for window in windows:
                keys = slice(window * BLK, (window + 1) * BLK)
                scores = dot_nt(win_k[keys, :], q_t)
                prob_grad = dot_nt(win_v[keys, :], g_t)
                w = jnp.exp2(scores * (scale * math.log2(math.e)))
                if window >= REACH:
                    w = jnp.where(ahead >= (window - REACH - slot_block[slot]) * BLK, w, 0.0)
                w_buf[unit, keys, :] = w
                d_buf[unit, keys, :] = prob_grad
                on = valid(slot, window)
                more = on * sub_sum(w)
                more_e = on * sub_sum(w * prob_grad)
                total = more if total is None else total + more
                total_e = more_e if total_e is None else total_e + more_e
            l_buf[unit] = total
            e_buf[unit] = total_e

    finished = {}

    def finish(unit):
        if unit not in finished:
            finished[unit] = normalise(unit)
        return finished[unit]

    def inverse_of(unit):
        total = jnp.sum(l_buf[unit], axis=0, keepdims=True)
        return jnp.where(total > 0.0, 1.0 / total, 0.0)

    def delta_of(unit, inverse):
        return jnp.sum(e_buf[unit], axis=0, keepdims=True) * inverse

    def normalise(unit):
        inverse = inverse_of(unit)
        return inverse, delta_of(unit, inverse)

    written = set()

    def grads(slot, windows):
        for unit in range(slot * UNITS, (slot + 1) * UNITS):
            at = slice(unit * UNIT, (unit + 1) * UNIT)
            q_t = q_all[at, :]
            g_t = g_all[at, :]
            inverse, delta = finish(unit)
            for window in windows:
                keys = slice(window * BLK, (window + 1) * BLK)
                attention = w_buf[unit, keys, :] * (inverse * valid(slot, window))
                score_grad = (attention * (d_buf[unit, keys, :] - delta)).astype(BF16)
                ds_buf[unit, keys, :] = score_grad
                part_k = dot_nn(score_grad, q_t)
                part_v = dot_nn(attention.astype(BF16), g_t)
                if window in written:
                    part_k = acc_k[keys, :] + part_k
                    part_v = acc_v[keys, :] + part_v
                written.add(window)
                acc_k[keys, :] = part_k
                acc_v[keys, :] = part_v

    def received(copies, windows, arrays):
        for away, window, array, copy in copies:
            if window in windows and array in arrays:

                @pl.when(me >= away)
                def _():
                    copy.wait_recv()

    def give_back(windows, arrays):
        for window in windows:
            keys = slice(window * BLK, (window + 1) * BLK)
            if 0 in arrays:
                out_k[keys, :] = (acc_k[keys, :] * scale).astype(BF16)
            if 1 in arrays:
                out_v[keys, :] = acc_v[keys, :].astype(BF16)
        for away, window, array, copy in back_copies:
            if window in windows and array in arrays:

                @pl.when(me >= away)
                def _():
                    copy.start()

    weigh(0, (4, 5), True)
    weigh(1, (4, 5, 6), True)
    received(halo_copies, (1, 2, 3), (0, 1))
    weigh(1, (1, 2, 3), False)
    weigh(0, (1, 2, 3), False)
    grads(1, (1, 2, 3))

    far = slice(0, BLK)
    units = range(UNITS)
    received(halo_copies, (0,), (0,))
    for unit in units:
        at = slice(unit * UNIT, (unit + 1) * UNIT)
        w = jnp.exp2(dot_nt(win_k[far, :], q_all[at, :]) * (scale * math.log2(math.e)))
        w_buf[unit, far, :] = w
        l_buf[unit] = l_buf[unit] + valid(0, 0) * sub_sum(w)
    inverses = [inverse_of(unit) for unit in units]

    def add(acc, window, part):
        keys = slice(window * BLK, (window + 1) * BLK)
        acc[keys, :] = part if window == 0 else acc[keys, :] + part

    def value_grads(window):
        keys = slice(window * BLK, (window + 1) * BLK)
        part = None
        for unit in units:
            at = slice(unit * UNIT, (unit + 1) * UNIT)
            attention = w_buf[unit, keys, :] * (inverses[unit] * valid(0, window))
            more = dot_nn(attention.astype(BF16), g_all[at, :])
            part = more if part is None else part + more
        add(acc_v, window, part)

    def key_grads(window):
        keys = slice(window * BLK, (window + 1) * BLK)
        part = None
        for unit in units:
            at = slice(unit * UNIT, (unit + 1) * UNIT)
            attention = w_buf[unit, keys, :] * (inverses[unit] * valid(0, window))
            score_grad = (attention * (d_buf[unit, keys, :] - deltas[unit])).astype(BF16)
            ds_buf[unit, keys, :] = score_grad
            more = dot_nn(score_grad, q_all[at, :])
            part = more if part is None else part + more
        add(acc_k, window, part)

    for window in (1, 2, 3):
        value_grads(window)
        give_back((window,), (1,))
    received(halo_copies, (0,), (1,))
    for unit in units:
        at = slice(unit * UNIT, (unit + 1) * UNIT)
        prob_grad = dot_nt(win_v[far, :], g_all[at, :])
        d_buf[unit, far, :] = prob_grad
        e_buf[unit] = e_buf[unit] + valid(0, 0) * sub_sum(w_buf[unit, far, :] * prob_grad)
    deltas = [delta_of(unit, inverses[unit]) for unit in units]
    for window in (1, 2, 3):
        key_grads(window)
        give_back((window,), (0,))
    value_grads(0)
    key_grads(0)
    give_back((0,), (0, 1))
    for unit in units:
        finished[unit] = (inverses[unit], deltas[unit])
    written.add(0)

    for window in range(WIN):
        keys = slice(window * BLK, (window + 1) * BLK)
        k_t[:, keys] = win_k[keys, :].T
    zero = jnp.zeros((), BF16)
    for slot, windows in ((0, (4, 5)), (1, (4, 5, 6))):
        grads(slot, windows)
        keys = slice(slot * BLK, (slot + WIN - 1) * BLK)
        for u in range(UNITS):
            part = dot_nn(k_t[:, keys], ds_buf[slot * UNITS + u, keys, :]) * scale
            both = jnp.concatenate([part[:, :BLK].T, part[:, BLK:].T], axis=1).astype(BF16)
            cols = slice(u * UNIT, (u + 1) * UNIT)
            is_low = slot_block[slot] == slot
            if slot == 0:
                dq_out[:BLK, cols] = jnp.where(is_low, both, zero)
                dq_out[BLK : 2 * BLK, cols] = jnp.where(is_low, zero, both)
            else:
                middle = dq_out[BLK : 2 * BLK, cols]
                take = is_low & (slot_live[1] == 1)
                dq_out[BLK : 2 * BLK, cols] = jnp.where(take, both, middle)
                dq_out[2 * BLK :, cols] = jnp.where(is_low, zero, both)

    for away, window, array, copy in back_copies:

        @pl.when(me + away < ranks)
        def _():
            copy.wait_recv()

    total_k = acc_k[halo:, :] * scale + near_k[...].astype(F32)
    total_v = acc_v[halo:, :] + near_v[...].astype(F32)
    last = (NB - 1) * BLK
    dk_out[:last, :] = total_k[:last].astype(BF16)
    dv_out[:last, :] = total_v[:last].astype(BF16)
    dk_out[last:, :] = (total_k[last:] + far_k[...].astype(F32)).astype(BF16)
    dv_out[last:, :] = (total_v[last:] + far_v[...].astype(F32)).astype(BF16)

    for away, window, array, copy in halo_copies:

        @pl.when(me + away < ranks)
        def _():
            copy.wait_send()

    for away, window, array, copy in back_copies:

        @pl.when(me >= away)
        def _():
            copy.wait_send()


def put_out(dq_in, dk_in, dv_in, dq_hbm, dk_hbm, dv_hbm, sem):
    copies = [
        pltpu.make_async_copy(dq_in, dq_hbm, sem.at[0]),
        pltpu.make_async_copy(dk_in, dk_hbm, sem.at[1]),
        pltpu.make_async_copy(dv_in, dv_hbm, sem.at[2]),
    ]
    for copy in copies:
        copy.start()
    for copy in copies:
        copy.wait()


def per_device(ranks, query_rows, key_rows, value_rows, out_grad, assistant, turn_first):
    rows = NB * BLK
    hbm = pl.BlockSpec(memory_space=pltpu.HBM)
    vmem = pl.BlockSpec(memory_space=pltpu.VMEM)
    units = 2 * UNITS
    scratch = [
        pltpu.VMEM((rows, SLOT), BF16),
        pltpu.VMEM((rows, SLOT), BF16),
        pltpu.VMEM((WIN * BLK, BLK), BF16),
        pltpu.VMEM((WIN * BLK, BLK), BF16),
        pltpu.VMEM((2 * SLOT, BLK), BF16),
        pltpu.VMEM((2 * SLOT, BLK), BF16),
        pltpu.VMEM((BLK, WIN * BLK), BF16),
        pltpu.VMEM((units, WIN * BLK, UNIT), F32),
        pltpu.VMEM((units, WIN * BLK, UNIT), F32),
        pltpu.VMEM((units, WIN * BLK, UNIT), BF16),
        pltpu.VMEM((units, 8, UNIT), F32),
        pltpu.VMEM((units, 8, UNIT), F32),
        pltpu.VMEM((WIN * BLK, BLK), F32),
        pltpu.VMEM((WIN * BLK, BLK), F32),
        pltpu.VMEM((REACH * BLK, BLK), BF16),
        pltpu.VMEM((REACH * BLK, BLK), BF16),
        pltpu.VMEM((rows, BLK), BF16),
        pltpu.VMEM((rows, BLK), BF16),
        pltpu.VMEM((BLK, BLK), BF16),
        pltpu.VMEM((BLK, BLK), BF16),
        pltpu.SMEM((1, assistant.shape[1]), jnp.int32),
        pltpu.SMEM((1, assistant.shape[1]), jnp.int32),
        pltpu.SemaphoreType.DMA((6,)),
        pltpu.SemaphoreType.DMA((8,)),
        pltpu.SemaphoreType.DMA((8,)),
        pltpu.SemaphoreType.DMA((8,)),
        pltpu.SemaphoreType.DMA((8,)),
    ]

    blocks = [
        pltpu.with_memory_space_constraint(x, pltpu.HBM)
        for x in (assistant, turn_first, query_rows[0], key_rows[0], value_rows[0], out_grad[0])
    ]

    def body(*refs):
        kernel(ranks, *refs)

    shapes = (
        jax.ShapeDtypeStruct((rows, SLOT), BF16),
        jax.ShapeDtypeStruct((rows, BLK), BF16),
        jax.ShapeDtypeStruct((rows, BLK), BF16),
    )
    held = pl.pallas_call(
        body,
        out_shape=shapes,
        in_specs=[hbm, hbm, hbm, hbm, hbm, hbm],
        out_specs=(vmem, vmem, vmem),
        scratch_shapes=scratch,
        compiler_params=pltpu.CompilerParams(
            collective_id=0, has_side_effects=True, vmem_limit_bytes=40 * 1024 * 1024
        ),
        name="attention_backward",
    )(*blocks)
    dq, dk, dv = pl.pallas_call(
        put_out,
        out_shape=shapes,
        in_specs=[vmem, vmem, vmem],
        out_specs=(hbm, hbm, hbm),
        scratch_shapes=[pltpu.SemaphoreType.DMA((3,))],
        compiler_params=pltpu.CompilerParams(vmem_limit_bytes=4 * 1024 * 1024),
        name="put_out",
    )(*held)
    return dq[None], dk[None], dv[None]


def solution(mesh):
    ranks = mesh.shape["ctx"]

    def step(*arrays):
        return per_device(ranks, *arrays)

    wide = P("dp", "ctx", "tp")
    return jax.shard_map(
        step,
        mesh=mesh,
        in_specs=(wide, wide, wide, wide, P("dp", None), P("dp", None)),
        out_specs=(wide, wide, wide),
        check_vma=False,
    )
```

```python
import math

import jax
import jax.numpy as jnp
from jax import lax
from jax.experimental import pallas as pl
from jax.experimental.pallas import tpu as pltpu
from jax.sharding import PartitionSpec as P

BLK = 128
QH = 8
NB = 3
REACH = 4
WIN = REACH + NB
SLOT = QH * BLK
UNIT = 2 * BLK
UNITS = SLOT // UNIT
MESH = pl.DeviceIdType.MESH
F32 = jnp.float32
BF16 = jnp.bfloat16


def dot_nt(a, b):
    return lax.dot_general(a, b, (((1,), (1,)), ((), ())), preferred_element_type=F32)


def dot_nn(a, b):
    return lax.dot_general(a, b, (((1,), (0,)), ((), ())), preferred_element_type=F32)


def sub_sum(x):
    return jnp.sum(x.reshape(x.shape[0] // 8, 8, x.shape[1]), axis=0)


def kernel(
    ranks,
    assist_hbm,
    first_hbm,
    q_hbm,
    k_hbm,
    v_hbm,
    g_hbm,
    dq_out,
    dk_out,
    dv_out,
    q_in,
    g_in,
    win_k,
    win_v,
    q_all,
    g_all,
    k_t,
    w_buf,
    d_buf,
    ds_buf,
    l_buf,
    e_buf,
    acc_k,
    acc_v,
    out_k,
    out_v,
    near_k,
    near_v,
    q_next,
    g_next,
    sum_out,
    sum_in,
    assist,
    first,
    in_sem,
    fs_sem,
    fr_sem,
    bs_sem,
    br_sem,
    ns_sem,
    nr_sem,
    here_sem,
):
    me = lax.axis_index("ctx")
    scale = 1.0 / math.sqrt(BLK)
    base = me * NB
    halo = REACH * BLK

    local = [
        pltpu.make_async_copy(k_hbm, win_k.at[pl.ds(halo, NB * BLK)], in_sem.at[0]),
        pltpu.make_async_copy(v_hbm, win_v.at[pl.ds(halo, NB * BLK)], in_sem.at[1]),
        pltpu.make_async_copy(q_hbm, q_in, in_sem.at[2]),
        pltpu.make_async_copy(g_hbm, g_in, in_sem.at[3]),
        pltpu.make_async_copy(assist_hbm, assist, in_sem.at[4]),
        pltpu.make_async_copy(first_hbm, first, in_sem.at[5]),
    ]
    def halo_copy(array, block, window, away, slot):
        src = (k_hbm, v_hbm)[array].at[pl.ds(block * BLK, BLK)]
        dst = (win_k, win_v)[array].at[pl.ds(window * BLK, BLK)]
        return pltpu.make_async_remote_copy(
            src_ref=src,
            dst_ref=dst,
            send_sem=fs_sem.at[slot],
            recv_sem=fr_sem.at[slot],
            device_id={"ctx": me + away},
            device_id_type=MESH,
        )

    halo_copies = []
    for window in (0, 1, 2, 3):
        away = 2 if window == 0 else 1
        block = NB - 1 if window == 0 else window - 1
        for array in (0, 1):
            halo_copies.append(
                (away, window, array, halo_copy(array, block, window, away, 2 * window + array))
            )

    back_copies = []
    for window in (1, 2, 3):
        for array in (0, 1):
            slot = 2 * (window - 1) + array
            copy = pltpu.make_async_remote_copy(
                src_ref=(out_k, out_v)[array].at[pl.ds(window * BLK, BLK)],
                dst_ref=(near_k, near_v)[array].at[pl.ds((window - 1) * BLK, BLK)],
                send_sem=bs_sem.at[slot],
                recv_sem=br_sem.at[slot],
                device_id={"ctx": me - 1},
                device_id_type=MESH,
            )
            back_copies.append((1, window, array, copy))

    lent = []
    for slot, (src, dst) in enumerate(
        (
            (q_hbm.at[pl.ds(0, BLK)], q_next),
            (g_hbm.at[pl.ds(0, BLK)], g_next),
            (sum_out, sum_in),
        )
    ):
        lent.append(
            pltpu.make_async_remote_copy(
                src_ref=src,
                dst_ref=dst,
                send_sem=ns_sem.at[slot],
                recv_sem=nr_sem.at[slot],
                device_id={"ctx": me - 1},
                device_id_type=MESH,
            )
        )

    barrier = pltpu.get_barrier_semaphore()
    for away in (1, 2):

        @pl.when(me >= away)
        def _():
            pl.semaphore_signal(
                barrier, inc=1, device_id={"ctx": me - away}, device_id_type=MESH
            )

    @pl.when(me < ranks - 1)
    def _():
        pl.semaphore_wait(barrier, jnp.minimum(ranks - 1 - me, 2))
        pl.semaphore_signal(
            here_sem, inc=1, device_id={"ctx": me + 1}, device_id_type=MESH
        )

    for away, window, array, copy in halo_copies:

        @pl.when(me + away < ranks)
        def _():
            copy.start()

    for copy in local:
        copy.start()

    for away, window, _, _ in halo_copies[::2]:

        @pl.when(me < away)
        def _():
            zero = jnp.zeros((BLK, BLK), BF16)
            win_k[window * BLK : (window + 1) * BLK, :] = zero
            win_v[window * BLK : (window + 1) * BLK, :] = zero

    @pl.when(me == ranks - 1)
    def _():
        near_k[...] = jnp.zeros_like(near_k)
        near_v[...] = jnp.zeros_like(near_v)
        q_next[...] = jnp.zeros_like(q_next)
        g_next[...] = jnp.zeros_like(g_next)
        sum_in[...] = jnp.zeros_like(sum_in)

    for copy in local:
        copy.wait()

    after = jnp.minimum(base + NB, ranks * NB - 1)
    mark = [assist[0, base + i] for i in range(NB)] + [assist[0, after]]
    turn = [first[0, base + i] for i in range(NB)] + [first[0, after]]
    head_is_first = mark[0] == 1
    tail_is_last = mark[2] == 1
    slot_block = (jnp.where(head_is_first, 0, 1), jnp.where(tail_is_last, 2, 1))
    slot_turn = (
        jnp.where(head_is_first, turn[0], turn[1]),
        jnp.where(tail_is_last, turn[2], turn[1]),
        turn[3],
    )
    slot_live = (
        jnp.maximum(mark[0], mark[1]),
        jnp.maximum(mark[2], mark[0] * mark[1]),
        jnp.where(me < ranks - 1, mark[3], 0),
    )

    def valid(slot, window):
        seen = (base - REACH + window >= slot_turn[slot]) & (slot_live[slot] == 1)
        return jnp.where(seen, jnp.float32(1.0), jnp.float32(0.0))

    for slot in (0, 1):
        low = slice(slot * BLK, (slot + 1) * BLK)
        high = slice((slot + 1) * BLK, (slot + 2) * BLK)
        for head in range(QH):
            at = slot * SLOT + head * BLK
            cols = slice(head * BLK, (head + 1) * BLK)
            is_low = slot_block[slot] == slot
            q_all[at : at + BLK, :] = jnp.where(is_low, q_in[low, cols], q_in[high, cols])
            g_all[at : at + BLK, :] = jnp.where(is_low, g_in[low, cols], g_in[high, cols])

    ahead = (lax.broadcasted_iota(jnp.int32, (BLK, UNIT), 1) % BLK) - lax.broadcasted_iota(
        jnp.int32, (BLK, UNIT), 0
    )

    def weigh(slot, windows, opens):
        for unit in range(slot * UNITS, (slot + 1) * UNITS):
            at = slice(unit * UNIT, (unit + 1) * UNIT)
            q_t = q_all[at, :]
            g_t = g_all[at, :]
            total = None if opens else l_buf[unit]
            total_e = None if opens else e_buf[unit]
            for window in windows:
                keys = slice(window * BLK, (window + 1) * BLK)
                scores = dot_nt(win_k[keys, :], q_t)
                prob_grad = dot_nt(win_v[keys, :], g_t)
                w = jnp.exp2(scores * (scale * math.log2(math.e)))
                if window >= REACH and slot < 2:
                    w = jnp.where(ahead >= (window - REACH - slot_block[slot]) * BLK, w, 0.0)
                w_buf[unit, keys, :] = w
                d_buf[unit, keys, :] = prob_grad
                on = valid(slot, window)
                more = on * sub_sum(w)
                more_e = on * sub_sum(w * prob_grad)
                if slot == 0 and window == REACH:
                    sum_out[0, unit] = more
                    sum_out[1, unit] = more_e
                total = more if total is None else total + more
                total_e = more_e if total_e is None else total_e + more_e
            l_buf[unit] = total
            e_buf[unit] = total_e

    def normalise(unit, lent_sums=None):
        total, total_e = l_buf[unit], e_buf[unit]
        if lent_sums is not None:
            total, total_e = total + lent_sums[0], total_e + lent_sums[1]
        total = jnp.sum(total, axis=0, keepdims=True)
        inverse = jnp.where(total > 0.0, 1.0 / total, 0.0)
        return inverse, jnp.sum(total_e, axis=0, keepdims=True) * inverse

    written = set()

    def grads(slot, windows, stats, factor=1.0, keep=True):
        for u in range(UNITS):
            unit = slot * UNITS + u
            at = slice(unit * UNIT, (unit + 1) * UNIT)
            q_t = q_all[at, :]
            g_t = g_all[at, :]
            inverse, delta = stats[u]
            for window in windows:
                keys = slice(window * BLK, (window + 1) * BLK)
                attention = w_buf[unit, keys, :] * (inverse * (valid(slot, window) * factor))
                score_grad = (attention * (d_buf[unit, keys, :] - delta)).astype(BF16)
                if keep:
                    ds_buf[unit, keys, :] = score_grad
                part_k = dot_nn(score_grad, q_t)
                part_v = dot_nn(attention.astype(BF16), g_t)
                if window in written:
                    part_k = acc_k[keys, :] + part_k
                    part_v = acc_v[keys, :] + part_v
                written.add(window)
                acc_k[keys, :] = part_k
                acc_v[keys, :] = part_v

    def received(copies, windows, arrays):
        for away, window, array, copy in copies:
            if window in windows and array in arrays:

                @pl.when(me >= away)
                def _():
                    copy.wait_recv()

    def give_back(windows):
        for window in windows:
            keys = slice(window * BLK, (window + 1) * BLK)
            out_k[keys, :] = (acc_k[keys, :] * scale).astype(BF16)
            out_v[keys, :] = acc_v[keys, :].astype(BF16)
        for away, window, array, copy in back_copies:
            if window in windows:

                @pl.when(me >= away)
                def _():
                    copy.start()

    weigh(0, (4, 5), True)
    weigh(1, (4, 5, 6), True)

    @pl.when(me >= 1)
    def _():
        pl.semaphore_wait(here_sem, 1)
        for copy in lent:
            copy.start()

    @pl.when(me < ranks - 1)
    def _():
        for copy in lent:
            copy.wait_recv()

    for head in range(QH):
        at = slice(2 * SLOT + head * BLK, 2 * SLOT + (head + 1) * BLK)
        cols = slice(head * BLK, (head + 1) * BLK)
        q_all[at, :] = q_next[:, cols]
        g_all[at, :] = g_next[:, cols]
    weigh(2, (4, 5, 6), True)

    received(halo_copies, (1, 2, 3), (0, 1))
    weigh(1, (1, 2, 3), False)
    weigh(0, (1, 2, 3), False)
    weigh(2, (3,), False)
    stats = [normalise(UNITS + u) for u in range(UNITS)]
    grads(1, (1, 2, 3), stats)
    near_stats = [normalise(u) for u in range(UNITS)]
    not_lent = jnp.where(head_is_first, jnp.float32(0.0), jnp.float32(1.0))
    grads(0, (1, 2, 3), near_stats, not_lent, False)
    next_stats = [
        normalise(2 * UNITS + u, (sum_in[0, u], sum_in[1, u])) for u in range(UNITS)
    ]
    grads(2, (3,), next_stats, 1.0, False)
    give_back((1, 2, 3))
    grads(2, (4, 5, 6), next_stats, 1.0, False)
    grads(1, (4, 5, 6), stats)

    received(halo_copies, (0,), (0, 1))
    weigh(0, (0,), False)
    full_stats = [normalise(u) for u in range(UNITS)]
    for u in range(UNITS):
        inverse, delta = full_stats[u]
        for window in (0, 1, 2, 3):
            keys = slice(window * BLK, (window + 1) * BLK)
            attention = w_buf[u, keys, :] * (inverse * valid(0, window))
            ds_buf[u, keys, :] = (attention * (d_buf[u, keys, :] - delta)).astype(BF16)
    grads(0, (4, 5), full_stats)

    for window in range(WIN):
        keys = slice(window * BLK, (window + 1) * BLK)
        k_t[:, keys] = win_k[keys, :].T
    zero = jnp.zeros((), BF16)
    for slot in (0, 1):
        keys = slice(slot * BLK, (slot + WIN - 1) * BLK)
        for u in range(UNITS):
            part = dot_nn(k_t[:, keys], ds_buf[slot * UNITS + u, keys, :]) * scale
            both = jnp.concatenate([part[:, :BLK].T, part[:, BLK:].T], axis=1).astype(BF16)
            cols = slice(u * UNIT, (u + 1) * UNIT)
            is_low = slot_block[slot] == slot
            if slot == 0:
                dq_out[:BLK, cols] = jnp.where(is_low, both, zero)
                dq_out[BLK : 2 * BLK, cols] = jnp.where(is_low, zero, both)
            else:
                middle = dq_out[BLK : 2 * BLK, cols]
                take = is_low & (slot_live[1] == 1)
                dq_out[BLK : 2 * BLK, cols] = jnp.where(take, both, middle)
                dq_out[2 * BLK :, cols] = jnp.where(is_low, zero, both)

    for away, window, array, copy in halo_copies:

        @pl.when(me + away < ranks)
        def _():
            copy.wait_send()

    for away, window, array, copy in back_copies:

        @pl.when(me >= away)
        def _():
            copy.wait_send()

    @pl.when(me >= 1)
    def _():
        for copy in lent:
            copy.wait_send()

    for away, window, array, copy in back_copies:

        @pl.when(me + away < ranks)
        def _():
            copy.wait_recv()

    dk_out[...] = (acc_k[halo:, :] * scale + near_k[...].astype(F32)).astype(BF16)
    dv_out[...] = (acc_v[halo:, :] + near_v[...].astype(F32)).astype(BF16)


def put_out(dq_in, dk_in, dv_in, dq_hbm, dk_hbm, dv_hbm, sem):
    copies = [
        pltpu.make_async_copy(dq_in, dq_hbm, sem.at[0]),
        pltpu.make_async_copy(dk_in, dk_hbm, sem.at[1]),
        pltpu.make_async_copy(dv_in, dv_hbm, sem.at[2]),
    ]
    for copy in copies:
        copy.start()
    for copy in copies:
        copy.wait()


def per_device(ranks, query_rows, key_rows, value_rows, out_grad, assistant, turn_first):
    rows = NB * BLK
    hbm = pl.BlockSpec(memory_space=pltpu.HBM)
    vmem = pl.BlockSpec(memory_space=pltpu.VMEM)
    units = 3 * UNITS
    scratch = [
        pltpu.VMEM((rows, SLOT), BF16),
        pltpu.VMEM((rows, SLOT), BF16),
        pltpu.VMEM((WIN * BLK, BLK), BF16),
        pltpu.VMEM((WIN * BLK, BLK), BF16),
        pltpu.VMEM((3 * SLOT, BLK), BF16),
        pltpu.VMEM((3 * SLOT, BLK), BF16),
        pltpu.VMEM((BLK, WIN * BLK), BF16),
        pltpu.VMEM((units, WIN * BLK, UNIT), F32),
        pltpu.VMEM((units, WIN * BLK, UNIT), F32),
        pltpu.VMEM((2 * UNITS, WIN * BLK, UNIT), BF16),
        pltpu.VMEM((units, 8, UNIT), F32),
        pltpu.VMEM((units, 8, UNIT), F32),
        pltpu.VMEM((WIN * BLK, BLK), F32),
        pltpu.VMEM((WIN * BLK, BLK), F32),
        pltpu.VMEM((REACH * BLK, BLK), BF16),
        pltpu.VMEM((REACH * BLK, BLK), BF16),
        pltpu.VMEM((rows, BLK), BF16),
        pltpu.VMEM((rows, BLK), BF16),
        pltpu.VMEM((BLK, SLOT), BF16),
        pltpu.VMEM((BLK, SLOT), BF16),
        pltpu.VMEM((2, UNITS, 8, UNIT), F32),
        pltpu.VMEM((2, UNITS, 8, UNIT), F32),
        pltpu.SMEM((1, assistant.shape[1]), jnp.int32),
        pltpu.SMEM((1, assistant.shape[1]), jnp.int32),
        pltpu.SemaphoreType.DMA((6,)),
        pltpu.SemaphoreType.DMA((8,)),
        pltpu.SemaphoreType.DMA((8,)),
        pltpu.SemaphoreType.DMA((6,)),
        pltpu.SemaphoreType.DMA((6,)),
        pltpu.SemaphoreType.DMA((3,)),
        pltpu.SemaphoreType.DMA((3,)),
        pltpu.SemaphoreType.REGULAR,
    ]

    blocks = [
        pltpu.with_memory_space_constraint(x, pltpu.HBM)
        for x in (assistant, turn_first, query_rows[0], key_rows[0], value_rows[0], out_grad[0])
    ]

    def body(*refs):
        kernel(ranks, *refs)

    shapes = (
        jax.ShapeDtypeStruct((rows, SLOT), BF16),
        jax.ShapeDtypeStruct((rows, BLK), BF16),
        jax.ShapeDtypeStruct((rows, BLK), BF16),
    )
    held = pl.pallas_call(
        body,
        out_shape=shapes,
        in_specs=[hbm, hbm, hbm, hbm, hbm, hbm],
        out_specs=(vmem, vmem, vmem),
        scratch_shapes=scratch,
        compiler_params=pltpu.CompilerParams(
            collective_id=0, has_side_effects=True, vmem_limit_bytes=44 * 1024 * 1024
        ),
        name="attention_backward",
    )(*blocks)
    dq, dk, dv = pl.pallas_call(
        put_out,
        out_shape=shapes,
        in_specs=[vmem, vmem, vmem],
        out_specs=(hbm, hbm, hbm),
        scratch_shapes=[pltpu.SemaphoreType.DMA((3,))],
        compiler_params=pltpu.CompilerParams(vmem_limit_bytes=4 * 1024 * 1024),
        name="put_out",
    )(*held)
    return dq[None], dk[None], dv[None]


def solution(mesh):
    ranks = mesh.shape["ctx"]

    def step(*arrays):
        return per_device(ranks, *arrays)

    wide = P("dp", "ctx", "tp")
    return jax.shard_map(
        step,
        mesh=mesh,
        in_specs=(wide, wide, wide, wide, P("dp", None), P("dp", None)),
        out_specs=(wide, wide, wide),
        check_vma=False,
    )
```

```python
import math

import jax
import jax.numpy as jnp
from jax import lax
from jax.experimental import pallas as pl
from jax.experimental.pallas import tpu as pltpu
from jax.sharding import PartitionSpec as P

BLK = 128
QH = 8
NB = 3
REACH = 4
WIN = REACH + NB
SLOT = QH * BLK
UNIT = 2 * BLK
UNITS = SLOT // UNIT
MESH = pl.DeviceIdType.MESH
F32 = jnp.float32
BF16 = jnp.bfloat16


def dot_nt(a, b):
    return lax.dot_general(a, b, (((1,), (1,)), ((), ())), preferred_element_type=F32)


def dot_nn(a, b):
    return lax.dot_general(a, b, (((1,), (0,)), ((), ())), preferred_element_type=F32)


def sub_sum(x):
    return jnp.sum(x.reshape(x.shape[0] // 8, 8, x.shape[1]), axis=0)


def kernel(
    ranks,
    assist_hbm,
    first_hbm,
    q_hbm,
    k_hbm,
    v_hbm,
    g_hbm,
    dq_out,
    dk_out,
    dv_out,
    q_in,
    g_in,
    win_k,
    win_v,
    q_all,
    g_all,
    k_t,
    w_buf,
    d_buf,
    ds_buf,
    l_buf,
    e_buf,
    acc_k,
    acc_v,
    out_k,
    out_v,
    near_k,
    near_v,
    q_next,
    g_next,
    sum_out,
    sum_in,
    assist,
    first,
    in_sem,
    fs_sem,
    fr_sem,
    bs_sem,
    br_sem,
    ns_sem,
    nr_sem,
    here_sem,
):
    me = lax.axis_index("ctx")
    scale = 1.0 / math.sqrt(BLK)
    base = me * NB
    halo = REACH * BLK

    local = [
        pltpu.make_async_copy(k_hbm, win_k.at[pl.ds(halo, NB * BLK)], in_sem.at[0]),
        pltpu.make_async_copy(v_hbm, win_v.at[pl.ds(halo, NB * BLK)], in_sem.at[1]),
        pltpu.make_async_copy(q_hbm, q_in, in_sem.at[2]),
        pltpu.make_async_copy(g_hbm, g_in, in_sem.at[3]),
        pltpu.make_async_copy(assist_hbm, assist, in_sem.at[4]),
        pltpu.make_async_copy(first_hbm, first, in_sem.at[5]),
    ]
    def halo_copy(array, block, window, away, slot):
        src = (k_hbm, v_hbm)[array].at[pl.ds(block * BLK, BLK)]
        dst = (win_k, win_v)[array].at[pl.ds(window * BLK, BLK)]
        return pltpu.make_async_remote_copy(
            src_ref=src,
            dst_ref=dst,
            send_sem=fs_sem.at[slot],
            recv_sem=fr_sem.at[slot],
            device_id={"ctx": me + away},
            device_id_type=MESH,
        )

    halo_copies = []
    for window in (0, 1, 2, 3):
        away = 2 if window == 0 else 1
        block = NB - 1 if window == 0 else window - 1
        for array in (0, 1):
            halo_copies.append(
                (away, window, array, halo_copy(array, block, window, away, 2 * window + array))
            )

    back_copies = []
    for window in (1, 2, 3):
        for array in (0, 1):
            slot = 2 * (window - 1) + array
            copy = pltpu.make_async_remote_copy(
                src_ref=(out_k, out_v)[array].at[pl.ds(window * BLK, BLK)],
                dst_ref=(near_k, near_v)[array].at[pl.ds((window - 1) * BLK, BLK)],
                send_sem=bs_sem.at[slot],
                recv_sem=br_sem.at[slot],
                device_id={"ctx": me - 1},
                device_id_type=MESH,
            )
            back_copies.append((1, window, array, copy))

    lent = []
    for slot, (src, dst) in enumerate(
        (
            (q_hbm.at[pl.ds(0, BLK)], q_next),
            (g_hbm.at[pl.ds(0, BLK)], g_next),
            (sum_out, sum_in),
        )
    ):
        lent.append(
            pltpu.make_async_remote_copy(
                src_ref=src,
                dst_ref=dst,
                send_sem=ns_sem.at[slot],
                recv_sem=nr_sem.at[slot],
                device_id={"ctx": me - 1},
                device_id_type=MESH,
            )
        )

    barrier = pltpu.get_barrier_semaphore()
    for away in (1, 2):

        @pl.when(me >= away)
        def _():
            pl.semaphore_signal(
                barrier, inc=1, device_id={"ctx": me - away}, device_id_type=MESH
            )

    @pl.when(me < ranks - 1)
    def _():
        pl.semaphore_wait(barrier, jnp.minimum(ranks - 1 - me, 2))
        pl.semaphore_signal(
            here_sem, inc=1, device_id={"ctx": me + 1}, device_id_type=MESH
        )

    for away, window, array, copy in halo_copies:

        @pl.when(me + away < ranks)
        def _():
            copy.start()

    for copy in local:
        copy.start()

    @pl.when((me >= 1) & (me % 2 == 0))
    def _():
        pl.semaphore_wait(here_sem, 1)
        for copy in lent[:2]:
            copy.start()

    for away, window, _, _ in halo_copies[::2]:

        @pl.when(me < away)
        def _():
            zero = jnp.zeros((BLK, BLK), BF16)
            win_k[window * BLK : (window + 1) * BLK, :] = zero
            win_v[window * BLK : (window + 1) * BLK, :] = zero

    @pl.when(me == ranks - 1)
    def _():
        near_k[...] = jnp.zeros_like(near_k)
        near_v[...] = jnp.zeros_like(near_v)
        q_next[...] = jnp.zeros_like(q_next)
        g_next[...] = jnp.zeros_like(g_next)
        sum_in[...] = jnp.zeros_like(sum_in)

    for copy in local:
        copy.wait()

    after = jnp.minimum(base + NB, ranks * NB - 1)
    mark = [assist[0, base + i] for i in range(NB)] + [assist[0, after]]
    turn = [first[0, base + i] for i in range(NB)] + [first[0, after]]
    head_is_first = mark[0] == 1
    tail_is_last = mark[2] == 1
    slot_block = (jnp.where(head_is_first, 0, 1), jnp.where(tail_is_last, 2, 1))
    slot_turn = (
        jnp.where(head_is_first, turn[0], turn[1]),
        jnp.where(tail_is_last, turn[2], turn[1]),
        turn[3],
    )
    slot_live = (
        jnp.maximum(mark[0], mark[1]),
        jnp.maximum(mark[2], mark[0] * mark[1]),
        jnp.where(me < ranks - 1, mark[3], 0),
    )

    def valid(slot, window):
        seen = (base - REACH + window >= slot_turn[slot]) & (slot_live[slot] == 1)
        return jnp.where(seen, jnp.float32(1.0), jnp.float32(0.0))

    for slot in (0, 1):
        low = slice(slot * BLK, (slot + 1) * BLK)
        high = slice((slot + 1) * BLK, (slot + 2) * BLK)
        for head in range(QH):
            at = slot * SLOT + head * BLK
            cols = slice(head * BLK, (head + 1) * BLK)
            is_low = slot_block[slot] == slot
            q_all[at : at + BLK, :] = jnp.where(is_low, q_in[low, cols], q_in[high, cols])
            g_all[at : at + BLK, :] = jnp.where(is_low, g_in[low, cols], g_in[high, cols])

    ahead = (lax.broadcasted_iota(jnp.int32, (BLK, UNIT), 1) % BLK) - lax.broadcasted_iota(
        jnp.int32, (BLK, UNIT), 0
    )

    def weigh(slot, windows, opens):
        for unit in range(slot * UNITS, (slot + 1) * UNITS):
            at = slice(unit * UNIT, (unit + 1) * UNIT)
            q_t = q_all[at, :]
            g_t = g_all[at, :]
            total = None if opens else l_buf[unit]
            total_e = None if opens else e_buf[unit]
            for window in windows:
                keys = slice(window * BLK, (window + 1) * BLK)
                scores = dot_nt(win_k[keys, :], q_t)
                prob_grad = dot_nt(win_v[keys, :], g_t)
                w = jnp.exp2(scores * (scale * math.log2(math.e)))
                if window >= REACH and slot < 2:
                    w = jnp.where(ahead >= (window - REACH - slot_block[slot]) * BLK, w, 0.0)
                w_buf[unit, keys, :] = w
                d_buf[unit, keys, :] = prob_grad
                on = valid(slot, window)
                more = on * sub_sum(w)
                more_e = on * sub_sum(w * prob_grad)
                if slot == 0 and window == REACH:
                    row = UNITS + unit
                    sum_out[unit : unit + 1, :] = jnp.sum(more, axis=0, keepdims=True)
                    sum_out[row : row + 1, :] = jnp.sum(more_e, axis=0, keepdims=True)
                total = more if total is None else total + more
                total_e = more_e if total_e is None else total_e + more_e
            l_buf[unit] = total
            e_buf[unit] = total_e

    def normalise(unit, lent_row=None):
        total = jnp.sum(l_buf[unit], axis=0, keepdims=True)
        total_e = jnp.sum(e_buf[unit], axis=0, keepdims=True)
        if lent_row is not None:
            row = UNITS + lent_row
            total = total + sum_in[lent_row : lent_row + 1, :]
            total_e = total_e + sum_in[row : row + 1, :]
        inverse = jnp.where(total > 0.0, 1.0 / total, 0.0)
        return inverse, total_e * inverse

    written = set()

    def grads(slot, windows, stats, factor=1.0, keep=True):
        for u in range(UNITS):
            unit = slot * UNITS + u
            at = slice(unit * UNIT, (unit + 1) * UNIT)
            q_t = q_all[at, :]
            g_t = g_all[at, :]
            inverse, delta = stats[u]
            for window in windows:
                keys = slice(window * BLK, (window + 1) * BLK)
                attention = w_buf[unit, keys, :] * (inverse * (valid(slot, window) * factor))
                score_grad = (attention * (d_buf[unit, keys, :] - delta)).astype(BF16)
                if keep:
                    ds_buf[unit, keys, :] = score_grad
                part_k = dot_nn(score_grad, q_t)
                part_v = dot_nn(attention.astype(BF16), g_t)
                if window in written:
                    part_k = acc_k[keys, :] + part_k
                    part_v = acc_v[keys, :] + part_v
                written.add(window)
                acc_k[keys, :] = part_k
                acc_v[keys, :] = part_v

    def received(copies, windows, arrays):
        for away, window, array, copy in copies:
            if window in windows and array in arrays:

                @pl.when(me >= away)
                def _():
                    copy.wait_recv()

    def give_back(windows):
        for window in windows:
            keys = slice(window * BLK, (window + 1) * BLK)
            out_k[keys, :] = (acc_k[keys, :] * scale).astype(BF16)
            out_v[keys, :] = acc_v[keys, :].astype(BF16)
        for away, window, array, copy in back_copies:
            if window in windows:

                @pl.when(me >= away)
                def _():
                    copy.start()

    weigh(0, (4, 5), True)
    weigh(1, (4, 5, 6), True)

    @pl.when(me % 2 == 1)
    def _():
        pl.semaphore_wait(here_sem, 1)
        for copy in lent[:2]:
            copy.start()

    @pl.when(me >= 1)
    def _():
        lent[2].start()

    @pl.when(me < ranks - 1)
    def _():
        for copy in lent:
            copy.wait_recv()

    for head in range(QH):
        at = slice(2 * SLOT + head * BLK, 2 * SLOT + (head + 1) * BLK)
        cols = slice(head * BLK, (head + 1) * BLK)
        q_all[at, :] = q_next[:, cols]
        g_all[at, :] = g_next[:, cols]
    weigh(2, (4, 5, 6), True)

    received(halo_copies, (1, 2, 3), (0, 1))
    weigh(1, (1, 2, 3), False)
    weigh(0, (1, 2, 3), False)
    weigh(2, (3,), False)
    stats = [normalise(UNITS + u) for u in range(UNITS)]
    grads(1, (1, 2, 3), stats)
    near_stats = [normalise(u) for u in range(UNITS)]
    not_lent = jnp.where(head_is_first, jnp.float32(0.0), jnp.float32(1.0))
    grads(0, (1, 2, 3), near_stats, not_lent, False)
    next_stats = [normalise(2 * UNITS + u, u) for u in range(UNITS)]
    grads(2, (3,), next_stats, 1.0, False)
    give_back((1, 2, 3))
    grads(2, (4, 5, 6), next_stats, 1.0, False)
    grads(1, (4, 5, 6), stats)

    received(halo_copies, (0,), (0, 1))
    weigh(0, (0,), False)
    full_stats = [normalise(u) for u in range(UNITS)]
    for u in range(UNITS):
        inverse, delta = full_stats[u]
        for window in (0, 1, 2, 3):
            keys = slice(window * BLK, (window + 1) * BLK)
            attention = w_buf[u, keys, :] * (inverse * valid(0, window))
            ds_buf[u, keys, :] = (attention * (d_buf[u, keys, :] - delta)).astype(BF16)
    grads(0, (4, 5), full_stats)

    for window in range(WIN):
        keys = slice(window * BLK, (window + 1) * BLK)
        k_t[:, keys] = win_k[keys, :].T
    zero = jnp.zeros((), BF16)
    for slot in (0, 1):
        keys = slice(slot * BLK, (slot + WIN - 1) * BLK)
        for u in range(UNITS):
            part = dot_nn(k_t[:, keys], ds_buf[slot * UNITS + u, keys, :]) * scale
            both = jnp.concatenate([part[:, :BLK].T, part[:, BLK:].T], axis=1).astype(BF16)
            cols = slice(u * UNIT, (u + 1) * UNIT)
            is_low = slot_block[slot] == slot
            if slot == 0:
                dq_out[:BLK, cols] = jnp.where(is_low, both, zero)
                dq_out[BLK : 2 * BLK, cols] = jnp.where(is_low, zero, both)
            else:
                middle = dq_out[BLK : 2 * BLK, cols]
                take = is_low & (slot_live[1] == 1)
                dq_out[BLK : 2 * BLK, cols] = jnp.where(take, both, middle)
                dq_out[2 * BLK :, cols] = jnp.where(is_low, zero, both)

    for away, window, array, copy in halo_copies:

        @pl.when(me + away < ranks)
        def _():
            copy.wait_send()

    for away, window, array, copy in back_copies:

        @pl.when(me >= away)
        def _():
            copy.wait_send()

    @pl.when(me >= 1)
    def _():
        for copy in lent:
            copy.wait_send()

    for away, window, array, copy in back_copies:

        @pl.when(me + away < ranks)
        def _():
            copy.wait_recv()

    dk_out[...] = (acc_k[halo:, :] * scale + near_k[...].astype(F32)).astype(BF16)
    dv_out[...] = (acc_v[halo:, :] + near_v[...].astype(F32)).astype(BF16)


def put_out(dq_in, dk_in, dv_in, dq_hbm, dk_hbm, dv_hbm, sem):
    copies = [
        pltpu.make_async_copy(dq_in, dq_hbm, sem.at[0]),
        pltpu.make_async_copy(dk_in, dk_hbm, sem.at[1]),
        pltpu.make_async_copy(dv_in, dv_hbm, sem.at[2]),
    ]
    for copy in copies:
        copy.start()
    for copy in copies:
        copy.wait()


def per_device(ranks, query_rows, key_rows, value_rows, out_grad, assistant, turn_first):
    rows = NB * BLK
    hbm = pl.BlockSpec(memory_space=pltpu.HBM)
    vmem = pl.BlockSpec(memory_space=pltpu.VMEM)
    units = 3 * UNITS
    scratch = [
        pltpu.VMEM((rows, SLOT), BF16),
        pltpu.VMEM((rows, SLOT), BF16),
        pltpu.VMEM((WIN * BLK, BLK), BF16),
        pltpu.VMEM((WIN * BLK, BLK), BF16),
        pltpu.VMEM((3 * SLOT, BLK), BF16),
        pltpu.VMEM((3 * SLOT, BLK), BF16),
        pltpu.VMEM((BLK, WIN * BLK), BF16),
        pltpu.VMEM((units, WIN * BLK, UNIT), F32),
        pltpu.VMEM((units, WIN * BLK, UNIT), F32),
        pltpu.VMEM((2 * UNITS, WIN * BLK, UNIT), BF16),
        pltpu.VMEM((units, 8, UNIT), F32),
        pltpu.VMEM((units, 8, UNIT), F32),
        pltpu.VMEM((WIN * BLK, BLK), F32),
        pltpu.VMEM((WIN * BLK, BLK), F32),
        pltpu.VMEM((REACH * BLK, BLK), BF16),
        pltpu.VMEM((REACH * BLK, BLK), BF16),
        pltpu.VMEM((rows, BLK), BF16),
        pltpu.VMEM((rows, BLK), BF16),
        pltpu.VMEM((BLK, SLOT), BF16),
        pltpu.VMEM((BLK, SLOT), BF16),
        pltpu.VMEM((2 * UNITS, UNIT), F32),
        pltpu.VMEM((2 * UNITS, UNIT), F32),
        pltpu.SMEM((1, assistant.shape[1]), jnp.int32),
        pltpu.SMEM((1, assistant.shape[1]), jnp.int32),
        pltpu.SemaphoreType.DMA((6,)),
        pltpu.SemaphoreType.DMA((8,)),
        pltpu.SemaphoreType.DMA((8,)),
        pltpu.SemaphoreType.DMA((6,)),
        pltpu.SemaphoreType.DMA((6,)),
        pltpu.SemaphoreType.DMA((3,)),
        pltpu.SemaphoreType.DMA((3,)),
        pltpu.SemaphoreType.REGULAR,
    ]

    blocks = [
        pltpu.with_memory_space_constraint(x, pltpu.HBM)
        for x in (assistant, turn_first, query_rows[0], key_rows[0], value_rows[0], out_grad[0])
    ]

    def body(*refs):
        kernel(ranks, *refs)

    shapes = (
        jax.ShapeDtypeStruct((rows, SLOT), BF16),
        jax.ShapeDtypeStruct((rows, BLK), BF16),
        jax.ShapeDtypeStruct((rows, BLK), BF16),
    )
    held = pl.pallas_call(
        body,
        out_shape=shapes,
        in_specs=[hbm, hbm, hbm, hbm, hbm, hbm],
        out_specs=(vmem, vmem, vmem),
        scratch_shapes=scratch,
        compiler_params=pltpu.CompilerParams(
            collective_id=0, has_side_effects=True, vmem_limit_bytes=44 * 1024 * 1024
        ),
        name="attention_backward",
    )(*blocks)
    dq, dk, dv = pl.pallas_call(
        put_out,
        out_shape=shapes,
        in_specs=[vmem, vmem, vmem],
        out_specs=(hbm, hbm, hbm),
        scratch_shapes=[pltpu.SemaphoreType.DMA((3,))],
        compiler_params=pltpu.CompilerParams(vmem_limit_bytes=4 * 1024 * 1024),
        name="put_out",
    )(*held)
    return dq[None], dk[None], dv[None]


def solution(mesh):
    ranks = mesh.shape["ctx"]

    def step(*arrays):
        return per_device(ranks, *arrays)

    wide = P("dp", "ctx", "tp")
    return jax.shard_map(
        step,
        mesh=mesh,
        in_specs=(wide, wide, wide, wide, P("dp", None), P("dp", None)),
        out_specs=(wide, wide, wide),
        check_vma=False,
    )
```

```python
import math

import jax
import jax.numpy as jnp
from jax import lax
from jax.experimental import pallas as pl
from jax.experimental.pallas import tpu as pltpu
from jax.sharding import PartitionSpec as P

BLK = 128
QH = 8
NB = 3
REACH = 4
WIN = REACH + NB
SLOT = QH * BLK
UNIT = 2 * BLK
UNITS = SLOT // UNIT
MESH = pl.DeviceIdType.MESH
F32 = jnp.float32
BF16 = jnp.bfloat16


def dot_nt(a, b):
    return lax.dot_general(a, b, (((1,), (1,)), ((), ())), preferred_element_type=F32)


def dot_nn(a, b):
    return lax.dot_general(a, b, (((1,), (0,)), ((), ())), preferred_element_type=F32)


def sub_sum(x):
    return jnp.sum(x.reshape(x.shape[0] // 8, 8, x.shape[1]), axis=0)


def kernel(
    ranks,
    assist_hbm,
    first_hbm,
    q_hbm,
    k_hbm,
    v_hbm,
    g_hbm,
    dq_out,
    dk_out,
    dv_out,
    q_in,
    g_in,
    win_k,
    win_v,
    q_all,
    g_all,
    k_t,
    w_buf,
    d_buf,
    ds_buf,
    l_buf,
    e_buf,
    acc_k,
    acc_v,
    out_k,
    out_v,
    near_k,
    near_v,
    q_next,
    g_next,
    sum_out,
    sum_in,
    assist,
    first,
    in_sem,
    fs_sem,
    fr_sem,
    bs_sem,
    br_sem,
    ns_sem,
    nr_sem,
    here_sem,
):
    me = lax.axis_index("ctx")
    scale = 1.0 / math.sqrt(BLK)
    base = me * NB
    halo = REACH * BLK

    local = [
        pltpu.make_async_copy(k_hbm, win_k.at[pl.ds(halo, NB * BLK)], in_sem.at[0]),
        pltpu.make_async_copy(v_hbm, win_v.at[pl.ds(halo, NB * BLK)], in_sem.at[1]),
        pltpu.make_async_copy(q_hbm, q_in, in_sem.at[2]),
        pltpu.make_async_copy(g_hbm, g_in, in_sem.at[3]),
        pltpu.make_async_copy(assist_hbm, assist, in_sem.at[4]),
        pltpu.make_async_copy(first_hbm, first, in_sem.at[5]),
    ]
    def halo_copy(array, block, window, away, slot):
        src = (k_hbm, v_hbm)[array].at[pl.ds(block * BLK, BLK)]
        dst = (win_k, win_v)[array].at[pl.ds(window * BLK, BLK)]
        return pltpu.make_async_remote_copy(
            src_ref=src,
            dst_ref=dst,
            send_sem=fs_sem.at[slot],
            recv_sem=fr_sem.at[slot],
            device_id={"ctx": me + away},
            device_id_type=MESH,
        )

    halo_copies = []
    for window in (0, 1, 2, 3):
        away = 2 if window == 0 else 1
        block = NB - 1 if window == 0 else window - 1
        for array in (0, 1):
            halo_copies.append(
                (away, window, array, halo_copy(array, block, window, away, 2 * window + array))
            )

    back_copies = []
    for window in (1, 2, 3):
        for array in (0, 1):
            slot = 2 * (window - 1) + array
            copy = pltpu.make_async_remote_copy(
                src_ref=(out_k, out_v)[array].at[pl.ds(window * BLK, BLK)],
                dst_ref=(near_k, near_v)[array].at[pl.ds((window - 1) * BLK, BLK)],
                send_sem=bs_sem.at[slot],
                recv_sem=br_sem.at[slot],
                device_id={"ctx": me - 1},
                device_id_type=MESH,
            )
            back_copies.append((1, window, array, copy))

    lent = []
    for slot, (src, dst) in enumerate(
        (
            (q_hbm.at[pl.ds(0, BLK)], q_next),
            (g_hbm.at[pl.ds(0, BLK)], g_next),
            (sum_out, sum_in),
        )
    ):
        lent.append(
            pltpu.make_async_remote_copy(
                src_ref=src,
                dst_ref=dst,
                send_sem=ns_sem.at[slot],
                recv_sem=nr_sem.at[slot],
                device_id={"ctx": me - 1},
                device_id_type=MESH,
            )
        )

    barrier = pltpu.get_barrier_semaphore()
    for away in (1, 2):

        @pl.when(me >= away)
        def _():
            pl.semaphore_signal(
                barrier, inc=1, device_id={"ctx": me - away}, device_id_type=MESH
            )

    @pl.when(me < ranks - 1)
    def _():
        pl.semaphore_wait(barrier, jnp.minimum(ranks - 1 - me, 2))
        pl.semaphore_signal(
            here_sem, inc=1, device_id={"ctx": me + 1}, device_id_type=MESH
        )

    for away, window, array, copy in halo_copies:

        @pl.when(me + away < ranks)
        def _():
            copy.start()

    for copy in local:
        copy.start()

    @pl.when((me >= 1) & (me % 2 == 0))
    def _():
        pl.semaphore_wait(here_sem, 1)
        for copy in lent[:2]:
            copy.start()

    for away, window, _, _ in halo_copies[::2]:

        @pl.when(me < away)
        def _():
            zero = jnp.zeros((BLK, BLK), BF16)
            win_k[window * BLK : (window + 1) * BLK, :] = zero
            win_v[window * BLK : (window + 1) * BLK, :] = zero

    @pl.when(me == ranks - 1)
    def _():
        near_k[...] = jnp.zeros_like(near_k)
        near_v[...] = jnp.zeros_like(near_v)
        q_next[...] = jnp.zeros_like(q_next)
        g_next[...] = jnp.zeros_like(g_next)
        sum_in[...] = jnp.zeros_like(sum_in)

    for copy in local:
        copy.wait()

    after = jnp.minimum(base + NB, ranks * NB - 1)
    mark = [assist[0, base + i] for i in range(NB)] + [assist[0, after]]
    turn = [first[0, base + i] for i in range(NB)] + [first[0, after]]
    head_is_first = mark[0] == 1
    tail_is_last = mark[2] == 1
    slot_block = (jnp.where(head_is_first, 0, 1), jnp.where(tail_is_last, 2, 1))
    slot_turn = (
        jnp.where(head_is_first, turn[0], turn[1]),
        jnp.where(tail_is_last, turn[2], turn[1]),
        turn[3],
    )
    slot_live = (
        jnp.maximum(mark[0], mark[1]),
        jnp.maximum(mark[2], mark[0] * mark[1]),
        jnp.where(me < ranks - 1, mark[3], 0),
    )

    def valid(slot, window):
        seen = (base - REACH + window >= slot_turn[slot]) & (slot_live[slot] == 1)
        return jnp.where(seen, jnp.float32(1.0), jnp.float32(0.0))

    for slot in (0, 1):
        low = slice(slot * BLK, (slot + 1) * BLK)
        high = slice((slot + 1) * BLK, (slot + 2) * BLK)
        for head in range(QH):
            at = slot * SLOT + head * BLK
            cols = slice(head * BLK, (head + 1) * BLK)
            is_low = slot_block[slot] == slot
            q_all[at : at + BLK, :] = jnp.where(is_low, q_in[low, cols], q_in[high, cols])
            g_all[at : at + BLK, :] = jnp.where(is_low, g_in[low, cols], g_in[high, cols])

    ahead = (lax.broadcasted_iota(jnp.int32, (BLK, UNIT), 1) % BLK) - lax.broadcasted_iota(
        jnp.int32, (BLK, UNIT), 0
    )

    def weigh(slot, windows, opens):
        for unit in range(slot * UNITS, (slot + 1) * UNITS):
            at = slice(unit * UNIT, (unit + 1) * UNIT)
            q_t = q_all[at, :]
            g_t = g_all[at, :]
            total = None if opens else l_buf[unit]
            total_e = None if opens else e_buf[unit]
            for window in windows:
                keys = slice(window * BLK, (window + 1) * BLK)
                scores = dot_nt(win_k[keys, :], q_t)
                prob_grad = dot_nt(win_v[keys, :], g_t)
                w = jnp.exp2(scores * (scale * math.log2(math.e)))
                if window >= REACH and slot < 2:
                    w = jnp.where(ahead >= (window - REACH - slot_block[slot]) * BLK, w, 0.0)
                w_buf[unit, keys, :] = w
                d_buf[unit, keys, :] = prob_grad
                on = valid(slot, window)
                more = on * sub_sum(w)
                more_e = on * sub_sum(w * prob_grad)
                if slot == 0 and window == REACH:
                    row = UNITS + unit
                    sum_out[unit : unit + 1, :] = jnp.sum(more, axis=0, keepdims=True)
                    sum_out[row : row + 1, :] = jnp.sum(more_e, axis=0, keepdims=True)
                total = more if total is None else total + more
                total_e = more_e if total_e is None else total_e + more_e
            l_buf[unit] = total
            e_buf[unit] = total_e

    def normalise(unit, lent_row=None):
        total = jnp.sum(l_buf[unit], axis=0, keepdims=True)
        total_e = jnp.sum(e_buf[unit], axis=0, keepdims=True)
        if lent_row is not None:
            row = UNITS + lent_row
            total = total + sum_in[lent_row : lent_row + 1, :]
            total_e = total_e + sum_in[row : row + 1, :]
        inverse = jnp.where(total > 0.0, 1.0 / total, 0.0)
        return inverse, total_e * inverse

    written = set()

    def grads(slot, windows, stats, factor=1.0, keep=True):
        for u in range(UNITS):
            unit = slot * UNITS + u
            at = slice(unit * UNIT, (unit + 1) * UNIT)
            q_t = q_all[at, :]
            g_t = g_all[at, :]
            inverse, delta = stats[u]
            for window in windows:
                keys = slice(window * BLK, (window + 1) * BLK)
                attention = w_buf[unit, keys, :] * (inverse * (valid(slot, window) * factor))
                score_grad = (attention * (d_buf[unit, keys, :] - delta)).astype(BF16)
                if keep:
                    ds_buf[unit, keys, :] = score_grad
                part_k = dot_nn(score_grad, q_t)
                part_v = dot_nn(attention.astype(BF16), g_t)
                if window in written:
                    part_k = acc_k[keys, :] + part_k
                    part_v = acc_v[keys, :] + part_v
                written.add(window)
                acc_k[keys, :] = part_k
                acc_v[keys, :] = part_v

    def received(copies, windows, arrays):
        for away, window, array, copy in copies:
            if window in windows and array in arrays:

                @pl.when(me >= away)
                def _():
                    copy.wait_recv()

    def give_back(windows):
        for window in windows:
            keys = slice(window * BLK, (window + 1) * BLK)
            out_k[keys, :] = (acc_k[keys, :] * scale).astype(BF16)
            out_v[keys, :] = acc_v[keys, :].astype(BF16)
        for away, window, array, copy in back_copies:
            if window in windows:

                @pl.when(me >= away)
                def _():
                    copy.start()

    weigh(0, (4, 5), True)
    weigh(1, (4, 5, 6), True)

    @pl.when(me % 2 == 1)
    def _():
        pl.semaphore_wait(here_sem, 1)
        for copy in lent[:2]:
            copy.start()

    @pl.when(me >= 1)
    def _():
        lent[2].start()

    @pl.when(me < ranks - 1)
    def _():
        for copy in lent:
            copy.wait_recv()

    for head in range(QH):
        at = slice(2 * SLOT + head * BLK, 2 * SLOT + (head + 1) * BLK)
        cols = slice(head * BLK, (head + 1) * BLK)
        q_all[at, :] = q_next[:, cols]
        g_all[at, :] = g_next[:, cols]
    weigh(2, (4, 5, 6), True)

    received(halo_copies, (1, 2, 3), (0, 1))
    weigh(1, (1, 2, 3), False)
    weigh(0, (1, 2, 3), False)
    weigh(2, (3,), False)
    stats = [normalise(UNITS + u) for u in range(UNITS)]
    grads(1, (1, 2, 3), stats)
    near_stats = [normalise(u) for u in range(UNITS)]
    not_lent = jnp.where(head_is_first, jnp.float32(0.0), jnp.float32(1.0))
    grads(0, (1, 2, 3), near_stats, not_lent, False)
    next_stats = [normalise(2 * UNITS + u, u) for u in range(UNITS)]
    grads(2, (3,), next_stats, 1.0, False)
    grads(2, (4, 5, 6), next_stats, 1.0, False)
    grads(1, (4, 5, 6), stats)
    give_back((1, 2, 3))

    received(halo_copies, (0,), (0, 1))
    weigh(0, (0,), False)
    full_stats = [normalise(u) for u in range(UNITS)]
    for u in range(UNITS):
        inverse, delta = full_stats[u]
        for window in (0, 1, 2, 3):
            keys = slice(window * BLK, (window + 1) * BLK)
            attention = w_buf[u, keys, :] * (inverse * valid(0, window))
            ds_buf[u, keys, :] = (attention * (d_buf[u, keys, :] - delta)).astype(BF16)
    grads(0, (4, 5), full_stats)

    for window in range(WIN):
        keys = slice(window * BLK, (window + 1) * BLK)
        k_t[:, keys] = win_k[keys, :].T
    zero = jnp.zeros((), BF16)
    for slot in (0, 1):
        keys = slice(slot * BLK, (slot + WIN - 1) * BLK)
        for u in range(UNITS):
            part = dot_nn(k_t[:, keys], ds_buf[slot * UNITS + u, keys, :]) * scale
            both = jnp.concatenate([part[:, :BLK].T, part[:, BLK:].T], axis=1).astype(BF16)
            cols = slice(u * UNIT, (u + 1) * UNIT)
            is_low = slot_block[slot] == slot
            if slot == 0:
                dq_out[:BLK, cols] = jnp.where(is_low, both, zero)
                dq_out[BLK : 2 * BLK, cols] = jnp.where(is_low, zero, both)
            else:
                middle = dq_out[BLK : 2 * BLK, cols]
                take = is_low & (slot_live[1] == 1)
                dq_out[BLK : 2 * BLK, cols] = jnp.where(take, both, middle)
                dq_out[2 * BLK :, cols] = jnp.where(is_low, zero, both)

    for away, window, array, copy in halo_copies:

        @pl.when(me + away < ranks)
        def _():
            copy.wait_send()

    for away, window, array, copy in back_copies:

        @pl.when(me >= away)
        def _():
            copy.wait_send()

    @pl.when(me >= 1)
    def _():
        for copy in lent:
            copy.wait_send()

    for away, window, array, copy in back_copies:

        @pl.when(me + away < ranks)
        def _():
            copy.wait_recv()

    dk_out[...] = (acc_k[halo:, :] * scale + near_k[...].astype(F32)).astype(BF16)
    dv_out[...] = (acc_v[halo:, :] + near_v[...].astype(F32)).astype(BF16)


def put_out(dq_in, dk_in, dv_in, dq_hbm, dk_hbm, dv_hbm, sem):
    copies = [
        pltpu.make_async_copy(dq_in, dq_hbm, sem.at[0]),
        pltpu.make_async_copy(dk_in, dk_hbm, sem.at[1]),
        pltpu.make_async_copy(dv_in, dv_hbm, sem.at[2]),
    ]
    for copy in copies:
        copy.start()
    for copy in copies:
        copy.wait()


def per_device(ranks, query_rows, key_rows, value_rows, out_grad, assistant, turn_first):
    rows = NB * BLK
    hbm = pl.BlockSpec(memory_space=pltpu.HBM)
    vmem = pl.BlockSpec(memory_space=pltpu.VMEM)
    units = 3 * UNITS
    scratch = [
        pltpu.VMEM((rows, SLOT), BF16),
        pltpu.VMEM((rows, SLOT), BF16),
        pltpu.VMEM((WIN * BLK, BLK), BF16),
        pltpu.VMEM((WIN * BLK, BLK), BF16),
        pltpu.VMEM((3 * SLOT, BLK), BF16),
        pltpu.VMEM((3 * SLOT, BLK), BF16),
        pltpu.VMEM((BLK, WIN * BLK), BF16),
        pltpu.VMEM((units, WIN * BLK, UNIT), F32),
        pltpu.VMEM((units, WIN * BLK, UNIT), F32),
        pltpu.VMEM((2 * UNITS, WIN * BLK, UNIT), BF16),
        pltpu.VMEM((units, 8, UNIT), F32),
        pltpu.VMEM((units, 8, UNIT), F32),
        pltpu.VMEM((WIN * BLK, BLK), F32),
        pltpu.VMEM((WIN * BLK, BLK), F32),
        pltpu.VMEM((REACH * BLK, BLK), BF16),
        pltpu.VMEM((REACH * BLK, BLK), BF16),
        pltpu.VMEM((rows, BLK), BF16),
        pltpu.VMEM((rows, BLK), BF16),
        pltpu.VMEM((BLK, SLOT), BF16),
        pltpu.VMEM((BLK, SLOT), BF16),
        pltpu.VMEM((2 * UNITS, UNIT), F32),
        pltpu.VMEM((2 * UNITS, UNIT), F32),
        pltpu.SMEM((1, assistant.shape[1]), jnp.int32),
        pltpu.SMEM((1, assistant.shape[1]), jnp.int32),
        pltpu.SemaphoreType.DMA((6,)),
        pltpu.SemaphoreType.DMA((8,)),
        pltpu.SemaphoreType.DMA((8,)),
        pltpu.SemaphoreType.DMA((6,)),
        pltpu.SemaphoreType.DMA((6,)),
        pltpu.SemaphoreType.DMA((3,)),
        pltpu.SemaphoreType.DMA((3,)),
        pltpu.SemaphoreType.REGULAR,
    ]

    blocks = [
        pltpu.with_memory_space_constraint(x, pltpu.HBM)
        for x in (assistant, turn_first, query_rows[0], key_rows[0], value_rows[0], out_grad[0])
    ]

    def body(*refs):
        kernel(ranks, *refs)

    shapes = (
        jax.ShapeDtypeStruct((rows, SLOT), BF16),
        jax.ShapeDtypeStruct((rows, BLK), BF16),
        jax.ShapeDtypeStruct((rows, BLK), BF16),
    )
    held = pl.pallas_call(
        body,
        out_shape=shapes,
        in_specs=[hbm, hbm, hbm, hbm, hbm, hbm],
        out_specs=(vmem, vmem, vmem),
        scratch_shapes=scratch,
        compiler_params=pltpu.CompilerParams(
            collective_id=0, has_side_effects=True, vmem_limit_bytes=44 * 1024 * 1024
        ),
        name="attention_backward",
    )(*blocks)
    dq, dk, dv = pl.pallas_call(
        put_out,
        out_shape=shapes,
        in_specs=[vmem, vmem, vmem],
        out_specs=(hbm, hbm, hbm),
        scratch_shapes=[pltpu.SemaphoreType.DMA((3,))],
        compiler_params=pltpu.CompilerParams(vmem_limit_bytes=4 * 1024 * 1024),
        name="put_out",
    )(*held)
    return dq[None], dk[None], dv[None]


def solution(mesh):
    ranks = mesh.shape["ctx"]

    def step(*arrays):
        return per_device(ranks, *arrays)

    wide = P("dp", "ctx", "tp")
    return jax.shard_map(
        step,
        mesh=mesh,
        in_specs=(wide, wide, wide, wide, P("dp", None), P("dp", None)),
        out_specs=(wide, wide, wide),
        check_vma=False,
    )
```
